32 devices in a mesh: gx: 8 (over y, x, core), gy: 4 (over z).
Axes of the slice: x: 2, y: 2, z: 4, core: 2. Of those that a mesh axis runs over, the one named last changes fastest.
Arguments:
- block_input: bfloat16 [32, 40, 56, 256], P(('gx', 'gy')), may hold values from 0 to 6, as said below
- mid_first: bfloat16 [32, 40, 3584], P(('gx', 'gy')), may hold values from 0 to 6, as said below
- mid_second: bfloat16 [32, 40, 3584], P(('gx', 'gy')), may hold values from 0 to 18, as said below
- out_grad: bfloat16 [32, 40, 56, 256], P(('gx', 'gy')), may hold values from -6 to 6
- params: float32 [64, 1088], replicated, may hold values from -18 to 18
- velocity: float32 [64, 1088], P('gx'), may hold values from -1.8 to 1.8
Outputs:
- input_grad: bfloat16 [32, 40, 56, 256], P(('gx', 'gy'))
- new_velocity: float32 [64, 1088], P('gx')
- next_weights: float32 [64, 1088], replicated
The draws below stay inside these ranges and needn't reach their ends.
Inputs may be any that keep to these rules, and one draw needn't show every extreme that they name: `block_input`: ReLU outputs: nonnegative, about half of the entries zero. `mid_first`: ReLU outputs: nonnegative, about half of the entries zero. `mid_second`: ReLU outputs: nonnegative, about half of the entries zero.
All inputs are finite; a program needn't handle non-finite values.
Results may differ from the reference program's by a relative error of at most 0.0074.
Values sent between devices are 32-bit elements; how exact they have to be, the bound alone decides.
No kernel may reach another device: no remote copies, remote signals or barrier semaphores. Data moves between devices by JAX's collectives and lax.ppermute only.
A program may use at most 64 MiB of HBM per device.

```python
import math
import jax
import jax.numpy as jnp
from jax import lax

C_IN = 256
C_MID = 64
H_DEV = 40
W_IMG = 56
K_ROW = 1088
STRIPS = 32


def relu_field(key, field_shape, channels, rising):
    key_base, key_scale = jax.random.split(key)
    base_draw = jax.random.truncated_normal(key_base, -4.0, 4.0, field_shape, jnp.float32)
    channel_scale = jnp.exp(jax.random.uniform(key_scale, (channels,), jnp.float32, math.log(0.5), math.log(1.5)))
    if rising:
        channel_scale = channel_scale * 3.0 ** (jnp.arange(channels, dtype=jnp.float32) / (channels - 1))
    return jnp.maximum(base_draw, 0.0) * channel_scale


def draw_block_input(key, part):
    field = relu_field(jax.random.fold_in(key, 11), (STRIPS, H_DEV, W_IMG, C_IN), C_IN, False)
    return field.astype(jnp.bfloat16)


def draw_mid_first(key, part):
    field = relu_field(jax.random.fold_in(key, 12), (STRIPS, H_DEV, W_IMG, C_MID), C_MID, False)
    return field.reshape(STRIPS, H_DEV, W_IMG * C_MID).astype(jnp.bfloat16)


def draw_mid_second(key, part):
    field = relu_field(jax.random.fold_in(key, 13), (STRIPS, H_DEV, W_IMG, C_MID), C_MID, True)
    return field.reshape(STRIPS, H_DEV, W_IMG * C_MID).astype(jnp.bfloat16)


def draw_params(key, part):
    key_base, key_scale = jax.random.split(jax.random.fold_in(key, 14))
    base_draw = jax.random.truncated_normal(key_base, -4.0, 4.0, (C_MID, K_ROW), jnp.float32)
    row_scale = jnp.exp(jax.random.uniform(key_scale, (C_MID,), jnp.float32, math.log(0.4), math.log(1.5)))
    row_scale = row_scale * 3.0 ** (jnp.arange(C_MID, dtype=jnp.float32) / (C_MID - 1))
    return base_draw * row_scale[:, None]


def block_levels(rng, extent, shards, low, high):
    level = 1.0
    for dim, blocks in shards:
        steps = jax.random.uniform(jax.random.fold_in(jax.random.fold_in(rng, 6), dim), (blocks,), jnp.float32, low / len(shards), high / len(shards))
        level = level * jnp.repeat(jnp.exp(steps), extent[dim] // blocks).reshape((-1,) + (1,) * (len(extent) - 1 - dim))
    return level


def scatter_about(own_key, extent, width, reach, cuts=(), kind=jnp.bfloat16):
    loudness = block_levels(own_key, extent, cuts, -0.22, 0.18) if cuts else 1.0
    values = jax.random.normal(own_key, extent, jnp.float32) * width * loudness
    return jnp.minimum(jnp.maximum(values, -reach), reach).astype(kind)


def setup_inputs(seed: int = 0) -> dict:
    seeds = jax.random.split(jax.random.key(seed), 7)
    block_input = draw_block_input(jax.random.fold_in(seeds[6], 71), 0)
    mid_first = draw_mid_first(jax.random.fold_in(seeds[6], 71), 0)
    mid_second = draw_mid_second(jax.random.fold_in(seeds[6], 71), 0)
    out_grad = scatter_about(seeds[3], (STRIPS, H_DEV, W_IMG, C_IN), 1.0, 6.0, ((0, 32),))
    params = draw_params(jax.random.fold_in(seeds[6], 71), 0)
    velocity = scatter_about(seeds[5], (C_MID, K_ROW), 0.3, 1.8, ((0, 8),), jnp.float32)
    return {"block_input": block_input, "mid_first": mid_first, "mid_second": mid_second, "out_grad": out_grad, "params": params, "velocity": velocity}


learn_rate = 0.5
momentum = 0.9
norm_eps = 1e-06

def tap_patches(field):
    img_height, img_width = (field.shape[0], field.shape[1])
    padded = jnp.pad(field, ((1, 1), (1, 1), (0, 0)))
    pieces = [padded[tap_row:tap_row + img_height, tap_col:tap_col + img_width] for tap_row in range(3) for tap_col in range(3)]
    return jnp.concatenate(pieces, axis=2).reshape(img_height * img_width, 9 * field.shape[2])

def tap_sum(spread):
    img_height, img_width = (spread.shape[0], spread.shape[1])
    padded = jnp.pad(spread, ((1, 1), (1, 1), (0, 0), (0, 0)))
    result = jnp.zeros((img_height, img_width, spread.shape[3]), jnp.float32)
    for tap_row in range(3):
        for tap_col in range(3):
            result = result + padded[2 - tap_row:2 - tap_row + img_height, 2 - tap_col:2 - tap_col + img_width, 3 * tap_row + tap_col]
    return result

def outer_sum(left, right):
    return lax.dot_general(left, right, (((0,), (0,)), ((), ())), preferred_element_type=jnp.float32)

def strip_backward(x_strip, first_strip, second_strip, grad_strip, weights):
    img_height, img_width = (x_strip.shape[0], x_strip.shape[1])
    pixels = img_height * img_width
    scale_one = 1.0 / math.sqrt(C_IN)
    scale_two = 1.0 / math.sqrt(9 * C_MID)
    scale_three = 1.0 / math.sqrt(C_MID)
    w_first = weights[:, :C_IN]
    w_second = weights[:, C_IN:C_IN + 9 * C_MID]
    w_third = weights[:, C_IN + 9 * C_MID:]
    input_flat = x_strip.reshape(pixels, C_IN)
    out_flat = grad_strip.reshape(pixels, C_IN)
    first_field = first_strip.reshape(img_height, img_width, C_MID)
    second_flat = second_strip.reshape(pixels, C_MID)
    back_second = lax.dot_general(out_flat, w_third, (((1,), (1,)), ((), ())), preferred_element_type=jnp.float32) * scale_three
    back_second = jnp.where(second_flat > 0, back_second, 0.0).astype(jnp.bfloat16)
    spread = jnp.dot(back_second, w_second, preferred_element_type=jnp.float32) * scale_two
    back_first = tap_sum(spread.reshape(img_height, img_width, 9, C_MID))
    back_first = jnp.where(first_field > 0, back_first, 0.0).astype(jnp.bfloat16).reshape(pixels, C_MID)
    input_grad = (out_flat.astype(jnp.float32) + scale_one * jnp.dot(back_first, w_first, preferred_element_type=jnp.float32)).astype(jnp.bfloat16)
    patches = tap_patches(first_field)
    term = jnp.concatenate([scale_one * outer_sum(back_first, input_flat), scale_two * outer_sum(back_second, patches), scale_three * outer_sum(second_flat, out_flat)], axis=1)
    return (input_grad.reshape(img_height, img_width, C_IN), term)

def layer_squares(matrix):
    return jnp.stack([jnp.sum(matrix[:, :C_IN] ** 2), jnp.sum(matrix[:, C_IN:C_IN + 9 * C_MID] ** 2), jnp.sum(matrix[:, C_IN + 9 * C_MID:] ** 2)])

def trust_columns(trust_ratio):
    return jnp.concatenate([jnp.broadcast_to(trust_ratio[0], (C_IN,)), jnp.broadcast_to(trust_ratio[1], (9 * C_MID,)), jnp.broadcast_to(trust_ratio[2], (C_IN,))])

def reference(block_input, mid_first, mid_second, out_grad, params, velocity):
    weights = params.astype(jnp.bfloat16)

    def step(grad_total, strip_items):
        input_grad, term = strip_backward(strip_items[0], strip_items[1], strip_items[2], strip_items[3], weights)
        return (grad_total + term, input_grad)
    grad_total, input_grads = lax.scan(step, jnp.zeros((C_MID, K_ROW), jnp.float32), (block_input, mid_first, mid_second, out_grad))
    grad_mean = grad_total / STRIPS
    trust_ratio = jnp.sqrt(layer_squares(params)) / (jnp.sqrt(layer_squares(grad_mean)) + norm_eps)
    new_velocity = momentum * velocity + learn_rate * trust_columns(trust_ratio)[None, :] * grad_mean
    next_weights = params - new_velocity
    return (input_grads, new_velocity, next_weights)
```

```python
import functools
import math

import jax
import jax.numpy as jnp
from jax import lax
from jax.experimental import pallas as pl
from jax.experimental.pallas import tpu as pltpu
from jax.sharding import PartitionSpec as P

learn_rate = 0.5
momentum = 0.9
norm_eps = 1e-06

F32 = jnp.float32
BF16 = jnp.bfloat16


def divisor_up_to(number, limit):
    return max(d for d in range(1, limit + 1) if number % d == 0)


def spread_pixels(src_ref, dst_ref, base, height, width, mid):
    low = lax.broadcasted_iota(jnp.int32, (height, 2 * mid), 1) < mid
    for pair in range(width // 2):
        slab = src_ref[:, 2 * mid * pair : 2 * mid * (pair + 1)].astype(F32)
        turned = pltpu.roll(slab, mid, 1)
        dst_ref[pl.ds(base + 2 * pair, height, stride=width), :] = jnp.where(low, slab, turned)
        dst_ref[pl.ds(base + 2 * pair + 1, height, stride=width), :] = jnp.where(low, turned, slab)


def grad_kernel(
    core_ref, x_ref, first_ref, second_ref, out_ref, params_ref,
    keep_ref, send_ref, back_ref,
    first_px, second_px, bs_px, spread_px, bs_cols, first_rows, second_bf, taps_ref,
    *, height, width, strips, rows,
):
    c_in = x_ref.shape[1]
    mid = params_ref.shape[0]
    pixels = height * width
    pad = 8
    s_one, s_two, s_three = (1.0 / math.sqrt(n) for n in (c_in, 9 * mid, mid))
    block_rows = divisor_up_to(height, 8)
    step = block_rows * width
    chunks = [slice(k * step, (k + 1) * step) for k in range(height // block_rows)]
    low = lax.broadcasted_iota(jnp.int32, (step, 2 * mid), 1) < mid
    column = lax.broadcasted_iota(jnp.int32, (step, 2 * mid), 0) % width

    w_all = params_ref[...].astype(BF16)
    w_third = w_all[:, c_in + 9 * mid :]
    w_third = jnp.concatenate([w_third, w_third], axis=0)
    taps_ref[...] = jnp.zeros_like(taps_ref)
    for r in range(3):
        for q in range(3):
            t = 3 * r + q
            taps_ref[q * mid : (q + 1) * mid, r * mid : (r + 1) * mid] = params_ref[
                :, c_in + t * mid : c_in + (t + 1) * mid
            ].astype(BF16)

    spread_pixels(second_ref, second_px, 0, height, width, mid)
    first_px[:width, :] = jnp.zeros((width, 2 * mid), F32)
    first_px[width + pixels :, :] = jnp.zeros((width, 2 * mid), F32)
    spread_pixels(first_ref, first_px, width, height, width, mid)

    for c in chunks:
        back = lax.dot_general(out_ref[c, :], w_third, (((1,), (1,)), ((), ())), preferred_element_type=F32)
        second = second_px[c, :]
        bs_px[pad + c.start : pad + c.stop, :] = jnp.where(second > 0, back * s_three, 0.0)
        second_bf[c, :] = second.astype(BF16)

    spread_px[:width, :] = jnp.zeros((width, 4 * mid), F32)
    spread_px[width + pixels :, :] = jnp.zeros((width, 4 * mid), F32)
    for c in chunks:
        here = bs_px[pad + c.start : pad + c.stop, :]
        after = jnp.where(column < width - 1, bs_px[pad + 1 + c.start : pad + 1 + c.stop, :], 0.0)
        before = jnp.where(column > 0, bs_px[pad - 1 + c.start : pad - 1 + c.stop, :], 0.0)
        cols = jnp.concatenate([jnp.where(low, after, here), before], axis=1).astype(BF16)
        bs_cols[c, :] = cols
        spread_px[width + c.start : width + c.stop, :] = jnp.dot(cols, taps_ref[...], preferred_element_type=F32)
        above = first_px[c, :]
        level = first_px[width + c.start : width + c.stop, :]
        below = first_px[2 * width + c.start : 2 * width + c.stop, :]
        first_rows[c, :] = jnp.concatenate([jnp.where(low, above, level), below], axis=1).astype(BF16)

    for c in chunks:
        top = spread_px[2 * width + c.start : 2 * width + c.stop, : 2 * mid]
        centre = pltpu.roll(spread_px[width + c.start : width + c.stop, : 2 * mid], mid, 1)
        bottom = spread_px[c, 2 * mid :]
        total = (top + centre + bottom) * s_two
        total = jnp.where(first_px[width + c.start : width + c.stop, :] > 0, total, 0.0)
        back_ref[c, :] = total[:, :mid].astype(BF16)

    def outer(left, right):
        return lax.dot_general(left, right, (((0,), (0,)), ((), ())), preferred_element_type=F32)

    grad_one = outer(back_ref[...], x_ref[...]) * (s_one / strips)
    grad_two = outer(bs_cols[...], first_rows[...]) * (s_two / strips)
    grad_three = outer(second_bf[...], out_ref[...])[:mid] * (s_three / strips)

    def put(ref, parity):
        for k in range(mid // (2 * rows)):
            lo = (2 * k + parity) * rows
            ref[k, :, :c_in] = grad_one[lo : lo + rows]
            for r in range(3):
                for q in range(3):
                    t = 3 * r + q
                    ref[k, :, c_in + t * mid : c_in + (t + 1) * mid] = grad_two[
                        q * mid + lo : q * mid + lo + rows, r * mid : (r + 1) * mid
                    ]
            ref[k, :, c_in + 9 * mid :] = grad_three[lo : lo + rows]

    for own in range(2):

        @pl.when(core_ref[0] == own)
        def _():
            put(keep_ref, own)
            put(send_ref, 1 - own)


def input_grad_kernel(back_ref, out_ref, params_ref, result_ref):
    c_in = out_ref.shape[1]
    w_first = params_ref[:, :c_in].astype(BF16)
    change = jnp.dot(back_ref[...], w_first, preferred_element_type=F32)
    result_ref[...] = (out_ref[...].astype(F32) + (1.0 / math.sqrt(c_in)) * change).astype(BF16)


def update_kernel(
    place_ref, own_ref, other_ref, own_velocity_ref, other_velocity_ref, params_ref,
    velocity_ref, weights_ref, *, c_in, mid,
):
    core = place_ref[0]
    pair = place_ref[1]
    halves, rows, width = own_ref.shape
    lane = lax.broadcasted_iota(jnp.int32, (1, 1, width), 2)
    edges = (0, c_in, c_in + 9 * mid, width)

    def column_squares(ref):
        return jnp.sum(jnp.sum(ref[...] ** 2, axis=0, keepdims=True), axis=1, keepdims=True)

    grad_squares = column_squares(own_ref) + column_squares(other_ref)
    param_squares = column_squares(params_ref)
    factor = jnp.zeros((1, 1, width), F32)
    for start, stop in zip(edges[:-1], edges[1:]):
        inside = jnp.logical_and(lane >= start, lane < stop)

        def total(squares):
            return jnp.sum(jnp.where(inside, squares, 0.0), axis=2, keepdims=True)

        trust = jnp.sqrt(total(param_squares)) / (jnp.sqrt(total(grad_squares)) + norm_eps)
        factor = jnp.where(inside, learn_rate * trust, factor)
    factor = factor[0]
    for k in range(halves):
        for parity, grad, speed in ((core, own_ref, own_velocity_ref), (1 - core, other_ref, other_velocity_ref)):
            tile = 2 * k + parity
            weights_ref[tile] = params_ref[tile] - (momentum * speed[k ^ pair] + factor * grad[k])
    velocity_ref[...] = momentum * own_velocity_ref[0] + factor * own_ref[pair]


def full_vmem(count):
    return [pl.BlockSpec(memory_space=pltpu.VMEM) for _ in range(count)]


def flip(value, axis, bit):
    return lax.ppermute(value, axis, [(i, i ^ bit) for i in range(lax.axis_size(axis))])


def sum_over(value, axis):
    size = lax.axis_size(axis)
    bit = 1
    while size % (2 * bit) == 0:
        value = value + flip(value, axis, bit)
        bit *= 2
    terms = [value]
    for turn in range(1, size // bit):
        terms.append(lax.ppermute(value, axis, [(i, (i + turn * bit) % size) for i in range(size)]))
    return sum(terms[1:], terms[0])


def shards(block_input, mid_first, mid_second, out_grad, params, velocity):
    _, height, width, c_in = block_input.shape
    mid, row = params.shape
    pixels = height * width
    group = lax.axis_size("gx")
    rows = mid // group
    halves = group // 2
    strips = group * lax.axis_size("gy")
    place = lax.axis_index("gx")
    core = place % 2
    pair = place // 2
    out_flat = out_grad.reshape(pixels, c_in)

    keep, send, back_first = pl.pallas_call(
        functools.partial(grad_kernel, height=height, width=width, strips=strips, rows=rows),
        out_shape=(
            jax.ShapeDtypeStruct((halves, rows, row), F32),
            jax.ShapeDtypeStruct((halves, rows, row), F32),
            jax.ShapeDtypeStruct((pixels, mid), BF16),
        ),
        in_specs=[pl.BlockSpec(memory_space=pltpu.SMEM)] + full_vmem(5),
        out_specs=tuple(full_vmem(3)),
        scratch_shapes=[
            pltpu.VMEM((pixels + 2 * width, 2 * mid), F32),
            pltpu.VMEM((pixels, 2 * mid), F32),
            pltpu.VMEM((pixels + 16, 2 * mid), F32),
            pltpu.VMEM((pixels + 2 * width, 4 * mid), F32),
            pltpu.VMEM((pixels, 4 * mid), BF16),
            pltpu.VMEM((pixels, 4 * mid), BF16),
            pltpu.VMEM((pixels, 2 * mid), BF16),
            pltpu.VMEM((4 * mid, 4 * mid), BF16),
        ],
        name="grads",
    )(
        core.reshape(1),
        block_input.reshape(pixels, c_in),
        mid_first.reshape(height, width * mid),
        mid_second.reshape(height, width * mid),
        out_flat,
        params,
    )

    block = pixels // 4
    input_grad = pl.pallas_call(
        input_grad_kernel,
        out_shape=jax.ShapeDtypeStruct((pixels, c_in), BF16),
        grid=(pixels // block,),
        in_specs=[
            pl.BlockSpec((block, mid), lambda i: (i, 0)),
            pl.BlockSpec((block, c_in), lambda i: (i, 0)),
            pl.BlockSpec((mid, row), lambda i: (0, 0)),
        ],
        out_specs=pl.BlockSpec((block, c_in), lambda i: (i, 0)),
        cost_estimate=pl.CostEstimate(
            flops=2 * pixels * mid * c_in, bytes_accessed=2 * pixels * (2 * c_in + mid), transcendentals=0
        ),
        name="input_grad",
    )(back_first, out_flat, params)

    total = keep + flip(send, "gx", 1)
    speeds = velocity.reshape(1, rows, row)
    bit = 2
    while bit < group:
        total = total + flip(total, "gx", bit)
        speeds = jnp.concatenate([speeds, flip(speeds, "gx", bit)], axis=0)
        bit *= 2
    total = sum_over(total, "gy")
    both = flip(jnp.concatenate([total, speeds], axis=0), "gx", 1)

    new_velocity, next_weights = pl.pallas_call(
        functools.partial(update_kernel, c_in=c_in, mid=mid),
        out_shape=(
            jax.ShapeDtypeStruct((rows, row), F32),
            jax.ShapeDtypeStruct((group, rows, row), F32),
        ),
        in_specs=[pl.BlockSpec(memory_space=pltpu.SMEM)] + full_vmem(5),
        out_specs=tuple(full_vmem(2)),
        name="update",
    )(
        jnp.stack([core, pair]),
        total,
        both[:halves],
        speeds,
        both[halves:],
        params.reshape(group, rows, row),
    )
    return (input_grad.reshape(1, height, width, c_in), new_velocity, next_weights.reshape(mid, row))


def solution(mesh):
    return jax.shard_map(
        shards,
        mesh=mesh,
        in_specs=(
            P(("gx", "gy"), None, None, None),
            P(("gx", "gy"), None, None),
            P(("gx", "gy"), None, None),
            P(("gx", "gy"), None, None, None),
            P(),
            P("gx", None),
        ),
        out_specs=(P(("gx", "gy"), None, None, None), P("gx", None), P()),
        check_vma=False,
    )
```

```python
import functools
import math

import jax
import jax.numpy as jnp
from jax import lax
from jax.experimental import pallas as pl
from jax.experimental.pallas import tpu as pltpu
from jax.sharding import PartitionSpec as P

learn_rate = 0.5
momentum = 0.9
norm_eps = 1e-06

F32 = jnp.float32
BF16 = jnp.bfloat16


def divisor_up_to(number, limit):
    return max(d for d in range(1, limit + 1) if number % d == 0)


def spread_pixels(src_ref, dst_ref, base, height, width, mid):
    low = lax.broadcasted_iota(jnp.int32, (height, 2 * mid), 1) < mid
    for pair in range(width // 2):
        slab = src_ref[:, 2 * mid * pair : 2 * mid * (pair + 1)].astype(F32)
        turned = pltpu.roll(slab, mid, 1)
        dst_ref[pl.ds(base + 2 * pair, height, stride=width), :] = jnp.where(low, slab, turned)
        dst_ref[pl.ds(base + 2 * pair + 1, height, stride=width), :] = jnp.where(low, turned, slab)


def grad_kernel(
    place_ref, x_ref, first_ref, second_ref, out_ref, params_ref,
    keep_ref, send_ref, back_ref,
    first_px, second_px, bs_px, spread_px, bs_cols, first_rows, second_bf, taps_ref,
    *, height, width, strips, rows,
):
    c_in = x_ref.shape[1]
    mid = params_ref.shape[0]
    pixels = height * width
    pad = 8
    s_one, s_two, s_three = (1.0 / math.sqrt(n) for n in (c_in, 9 * mid, mid))
    block_rows = divisor_up_to(height, 8)
    step = block_rows * width
    chunks = [slice(k * step, (k + 1) * step) for k in range(height // block_rows)]
    low = lax.broadcasted_iota(jnp.int32, (step, 2 * mid), 1) < mid
    column = lax.broadcasted_iota(jnp.int32, (step, 2 * mid), 0) % width

    w_all = params_ref[...].astype(BF16)
    w_third = w_all[:, c_in + 9 * mid :]
    w_third = jnp.concatenate([w_third, w_third], axis=0)
    taps_ref[...] = jnp.zeros_like(taps_ref)
    for r in range(3):
        for q in range(3):
            t = 3 * r + q
            taps_ref[q * mid : (q + 1) * mid, r * mid : (r + 1) * mid] = params_ref[
                :, c_in + t * mid : c_in + (t + 1) * mid
            ].astype(BF16)

    spread_pixels(second_ref, second_px, 0, height, width, mid)
    first_px[:width, :] = jnp.zeros((width, 2 * mid), F32)
    first_px[width + pixels :, :] = jnp.zeros((width, 2 * mid), F32)
    spread_pixels(first_ref, first_px, width, height, width, mid)

    for c in chunks:
        back = lax.dot_general(out_ref[c, :], w_third, (((1,), (1,)), ((), ())), preferred_element_type=F32)
        second = second_px[c, :]
        bs_px[pad + c.start : pad + c.stop, :] = jnp.where(second > 0, back * s_three, 0.0)
        second_bf[c, :] = second.astype(BF16)

    spread_px[:width, :] = jnp.zeros((width, 4 * mid), F32)
    spread_px[width + pixels :, :] = jnp.zeros((width, 4 * mid), F32)
    for c in chunks:
        here = bs_px[pad + c.start : pad + c.stop, :]
        after = jnp.where(column < width - 1, bs_px[pad + 1 + c.start : pad + 1 + c.stop, :], 0.0)
        before = jnp.where(column > 0, bs_px[pad - 1 + c.start : pad - 1 + c.stop, :], 0.0)
        cols = jnp.concatenate([jnp.where(low, after, here), before], axis=1).astype(BF16)
        bs_cols[c, :] = cols
        spread_px[width + c.start : width + c.stop, :] = jnp.dot(cols, taps_ref[...], preferred_element_type=F32)
        above = first_px[c, :]
        level = first_px[width + c.start : width + c.stop, :]
        below = first_px[2 * width + c.start : 2 * width + c.stop, :]
        first_rows[c, :] = jnp.concatenate([jnp.where(low, above, level), below], axis=1).astype(BF16)

    for c in chunks:
        top = spread_px[2 * width + c.start : 2 * width + c.stop, : 2 * mid]
        centre = pltpu.roll(spread_px[width + c.start : width + c.stop, : 2 * mid], mid, 1)
        bottom = spread_px[c, 2 * mid :]
        total = (top + centre + bottom) * s_two
        total = jnp.where(first_px[width + c.start : width + c.stop, :] > 0, total, 0.0)
        back_ref[c, :] = total[:, :mid].astype(BF16)

    def outer(left, right):
        return lax.dot_general(left, right, (((0,), (0,)), ((), ())), preferred_element_type=F32)

    grad_one = outer(back_ref[...], x_ref[...]) * (s_one / strips)
    grad_two = outer(bs_cols[...], first_rows[...]) * (s_two / strips)
    grad_three = outer(second_bf[...], out_ref[...])[:mid] * (s_three / strips)

    def put(ref, parity):
        for k in range(mid // (2 * rows)):
            lo = (2 * k + parity) * rows
            ref[k, :, :c_in] = grad_one[lo : lo + rows]
            for r in range(3):
                for q in range(3):
                    t = 3 * r + q
                    ref[k, :, c_in + t * mid : c_in + (t + 1) * mid] = grad_two[
                        q * mid + lo : q * mid + lo + rows, r * mid : (r + 1) * mid
                    ]
            ref[k, :, c_in + 9 * mid :] = grad_three[lo : lo + rows]

    for own in range(2):

        @pl.when(place_ref[0] % 2 == own)
        def _():
            put(keep_ref, own)
            put(send_ref, 1 - own)


def input_grad_kernel(back_ref, out_ref, params_ref, *rest):
    result_ref = rest[-1]
    c_in = out_ref.shape[1]
    w_first = params_ref[:, :c_in].astype(BF16)
    change = jnp.dot(back_ref[...], w_first, preferred_element_type=F32)
    result_ref[...] = (out_ref[...].astype(F32) + (1.0 / math.sqrt(c_in)) * change).astype(BF16)


def update_kernel(
    place_ref, own_ref, other_ref, own_speed_ref, other_speed_ref, params_ref,
    velocity_ref, weights_ref, *, c_in, mid,
):
    core = place_ref[0] % 2
    pair = place_ref[0] // 2
    halves, rows, width = own_ref.shape
    lane = lax.broadcasted_iota(jnp.int32, (1, 1, width), 2)
    edges = (0, c_in, c_in + 9 * mid, width)

    def column_squares(ref):
        return jnp.sum(jnp.sum(ref[...] ** 2, axis=0, keepdims=True), axis=1, keepdims=True)

    grad_squares = column_squares(own_ref) + column_squares(other_ref)
    param_squares = column_squares(params_ref)
    factor = jnp.zeros((1, 1, width), F32)
    for start, stop in zip(edges[:-1], edges[1:]):
        inside = jnp.logical_and(lane >= start, lane < stop)

        def total(squares):
            return jnp.sum(jnp.where(inside, squares, 0.0), axis=2, keepdims=True)

        trust = jnp.sqrt(total(param_squares)) / (jnp.sqrt(total(grad_squares)) + norm_eps)
        factor = jnp.where(inside, learn_rate * trust, factor)
    factor = factor[0]
    for k in range(halves):
        for parity, grad, speed in ((core, own_ref, own_speed_ref), (1 - core, other_ref, other_speed_ref)):
            tile = 2 * k + parity
            weights_ref[tile] = params_ref[tile] - (momentum * speed[k ^ pair] + factor * grad[k])
    velocity_ref[...] = momentum * own_speed_ref[0] + factor * own_ref[pair]


def full_vmem(count):
    return [pl.BlockSpec(memory_space=pltpu.VMEM) for _ in range(count)]


def in_vmem(*arrays):
    return [pltpu.with_memory_space_constraint(a, pltpu.VMEM) for a in arrays]


def flip(value, axis, bit):
    return lax.ppermute(value, axis, [(i, i ^ bit) for i in range(lax.axis_size(axis))])


def exchange_steps(group, depth):
    across = [(0, 1 << b) for b in range(1, group.bit_length() - 1)]
    along = []
    bit = 1
    while depth % (2 * bit) == 0:
        along.append((1, bit))
        bit *= 2
    steps = []
    for one, two in zip(across, along):
        steps += [(one, two), (two, one)]
    common = min(len(across), len(along))
    steps += [(one, one) for one in across[common:] + along[common:]]
    pairs = []
    for step in steps:
        table = []
        for g in range(group):
            for z in range(depth):
                axis, flipped = step[g % 2]
                to_g, to_z = (g ^ flipped, z) if axis == 0 else (g, z ^ flipped)
                table.append((g * depth + z, to_g * depth + to_z))
        pairs.append(table)
    return pairs, bit


def shards(block_input, mid_first, mid_second, out_grad, params, velocity):
    _, height, width, c_in = block_input.shape
    mid, row = params.shape
    pixels = height * width
    group = lax.axis_size("gx")
    depth = lax.axis_size("gy")
    rows = mid // group
    halves = group // 2
    strips = group * depth
    place = lax.axis_index("gx").reshape(1)
    out_flat = out_grad.reshape(pixels, c_in)
    half = pltpu.VMEM((halves, rows, row), F32)

    keep, send, back_first = pl.pallas_call(
        functools.partial(grad_kernel, height=height, width=width, strips=strips, rows=rows),
        out_shape=(half, half, pltpu.VMEM((pixels, mid), BF16)),
        in_specs=[pl.BlockSpec(memory_space=pltpu.SMEM)] + full_vmem(5),
        out_specs=tuple(full_vmem(3)),
        scratch_shapes=[
            pltpu.VMEM((pixels + 2 * width, 2 * mid), F32),
            pltpu.VMEM((pixels, 2 * mid), F32),
            pltpu.VMEM((pixels + 16, 2 * mid), F32),
            pltpu.VMEM((pixels + 2 * width, 4 * mid), F32),
            pltpu.VMEM((pixels, 4 * mid), BF16),
            pltpu.VMEM((pixels, 4 * mid), BF16),
            pltpu.VMEM((pixels, 2 * mid), BF16),
            pltpu.VMEM((4 * mid, 4 * mid), BF16),
        ],
        name="grads",
    )(
        place,
        block_input.reshape(pixels, c_in),
        mid_first.reshape(height, width * mid),
        mid_second.reshape(height, width * mid),
        out_flat,
        params,
    )

    pieces = 2
    block = pixels // (2 * pieces)

    def input_grad_piece(piece, earlier):
        first = 2 * piece
        operands = [back_first, out_flat, params] + ([] if earlier is None else [earlier])
        return pl.pallas_call(
            input_grad_kernel,
            out_shape=jax.ShapeDtypeStruct((pixels, c_in), BF16),
            grid=(2,),
            in_specs=[
                pl.BlockSpec((block, mid), lambda i: (first + i, 0)),
                pl.BlockSpec((block, c_in), lambda i: (first + i, 0)),
                pl.BlockSpec((mid, row), lambda i: (0, 0)),
                pl.BlockSpec(memory_space=pl.ANY),
            ][: len(operands)],
            out_specs=pl.BlockSpec((block, c_in), lambda i: (first + i, 0)),
            input_output_aliases={} if earlier is None else {3: 0},
            cost_estimate=pl.CostEstimate(
                flops=2 * pixels * mid * c_in // pieces,
                bytes_accessed=2 * pixels * (2 * c_in + mid) // pieces,
                transcendentals=0,
            ),
            name="input_grad",
        )(*operands)

    total = keep + flip(send, "gx", 1)
    speeds = velocity.reshape(1, rows, row)
    bit = 2
    while bit < group:
        speeds = jnp.concatenate([speeds, flip(speeds, "gx", bit)], axis=0)
        bit *= 2
    other_speeds = flip(speeds, "gx", 1)
    input_grad = None
    steps, bit = exchange_steps(group, depth)
    for number, table in enumerate(steps):
        total = total + lax.ppermute(total, ("gx", "gy"), table)
        if number < pieces:
            input_grad = input_grad_piece(number, input_grad)
            total, input_grad = lax.optimization_barrier((total, input_grad))
    turned = [
        lax.ppermute(total, "gy", [(i, (i + turn * bit) % depth) for i in range(depth)])
        for turn in range(1, depth // bit)
    ]
    total = sum(turned, total)
    other = flip(total, "gx", 1)

    new_velocity, next_weights = pl.pallas_call(
        functools.partial(update_kernel, c_in=c_in, mid=mid),
        out_shape=(
            jax.ShapeDtypeStruct((rows, row), F32),
            jax.ShapeDtypeStruct((group, rows, row), F32),
        ),
        in_specs=[pl.BlockSpec(memory_space=pltpu.SMEM)] + full_vmem(5),
        out_specs=tuple(full_vmem(2)),
        name="update",
    )(place, *in_vmem(total, other, speeds, other_speeds, params.reshape(group, rows, row)))
    return (input_grad.reshape(1, height, width, c_in), new_velocity, next_weights.reshape(mid, row))


def solution(mesh):
    return jax.shard_map(
        shards,
        mesh=mesh,
        in_specs=(
            P(("gx", "gy"), None, None, None),
            P(("gx", "gy"), None, None),
            P(("gx", "gy"), None, None),
            P(("gx", "gy"), None, None, None),
            P(),
            P("gx", None),
        ),
        out_specs=(P(("gx", "gy"), None, None, None), P("gx", None), P()),
        check_vma=False,
    )
```

```python
import functools
import math

import jax
import jax.numpy as jnp
from jax import lax
from jax.experimental import pallas as pl
from jax.experimental.pallas import tpu as pltpu
from jax.sharding import PartitionSpec as P

learn_rate = 0.5
momentum = 0.9
norm_eps = 1e-06

F32 = jnp.float32
BF16 = jnp.bfloat16


def divisor_up_to(number, limit):
    return max(d for d in range(1, limit + 1) if number % d == 0)


def spread_pixels(src_ref, dst_ref, base, height, width, mid):
    low = lax.broadcasted_iota(jnp.int32, (height, 2 * mid), 1) < mid
    for pair in range(width // 2):
        slab = src_ref[:, 2 * mid * pair : 2 * mid * (pair + 1)].astype(F32)
        turned = pltpu.roll(slab, mid, 1)
        dst_ref[pl.ds(base + 2 * pair, height, stride=width), :] = jnp.where(low, slab, turned)
        dst_ref[pl.ds(base + 2 * pair + 1, height, stride=width), :] = jnp.where(low, turned, slab)


def grad_kernel(
    place_ref, x_ref, first_ref, second_ref, out_ref, params_ref,
    keep_ref, send_ref, back_ref,
    first_px, second_px, bs_px, spread_px, bs_cols, first_rows, second_bf, taps_ref,
    *, height, width, strips, rows,
):
    c_in = x_ref.shape[1]
    mid = params_ref.shape[0]
    pixels = height * width
    pad = 8
    s_one, s_two, s_three = (1.0 / math.sqrt(n) for n in (c_in, 9 * mid, mid))
    block_rows = divisor_up_to(height, 8)
    step = block_rows * width
    chunks = [slice(k * step, (k + 1) * step) for k in range(height // block_rows)]
    low = lax.broadcasted_iota(jnp.int32, (step, 2 * mid), 1) < mid
    column = lax.broadcasted_iota(jnp.int32, (step, 2 * mid), 0) % width

    w_all = params_ref[...].astype(BF16)
    w_third = w_all[:, c_in + 9 * mid :]
    w_third = jnp.concatenate([w_third, w_third], axis=0)
    taps_ref[...] = jnp.zeros_like(taps_ref)
    for r in range(3):
        for q in range(3):
            t = 3 * r + q
            taps_ref[q * mid : (q + 1) * mid, r * mid : (r + 1) * mid] = params_ref[
                :, c_in + t * mid : c_in + (t + 1) * mid
            ].astype(BF16)

    spread_pixels(second_ref, second_px, 0, height, width, mid)
    first_px[:width, :] = jnp.zeros((width, 2 * mid), F32)
    first_px[width + pixels :, :] = jnp.zeros((width, 2 * mid), F32)
    spread_pixels(first_ref, first_px, width, height, width, mid)

    for c in chunks:
        back = lax.dot_general(out_ref[c, :], w_third, (((1,), (1,)), ((), ())), preferred_element_type=F32)
        second = second_px[c, :]
        bs_px[pad + c.start : pad + c.stop, :] = jnp.where(second > 0, back * s_three, 0.0)
        second_bf[c, :] = second.astype(BF16)

    spread_px[:width, :] = jnp.zeros((width, 4 * mid), F32)
    spread_px[width + pixels :, :] = jnp.zeros((width, 4 * mid), F32)
    for c in chunks:
        here = bs_px[pad + c.start : pad + c.stop, :]
        after = jnp.where(column < width - 1, bs_px[pad + 1 + c.start : pad + 1 + c.stop, :], 0.0)
        before = jnp.where(column > 0, bs_px[pad - 1 + c.start : pad - 1 + c.stop, :], 0.0)
        cols = jnp.concatenate([jnp.where(low, after, here), before], axis=1).astype(BF16)
        bs_cols[c, :] = cols
        spread_px[width + c.start : width + c.stop, :] = jnp.dot(cols, taps_ref[...], preferred_element_type=F32)
        above = first_px[c, :]
        level = first_px[width + c.start : width + c.stop, :]
        below = first_px[2 * width + c.start : 2 * width + c.stop, :]
        first_rows[c, :] = jnp.concatenate([jnp.where(low, above, level), below], axis=1).astype(BF16)

    for c in chunks:
        top = spread_px[2 * width + c.start : 2 * width + c.stop, : 2 * mid]
        centre = pltpu.roll(spread_px[width + c.start : width + c.stop, : 2 * mid], mid, 1)
        bottom = spread_px[c, 2 * mid :]
        total = (top + centre + bottom) * s_two
        total = jnp.where(first_px[width + c.start : width + c.stop, :] > 0, total, 0.0)
        back_ref[c, :] = total[:, :mid].astype(BF16)

    def outer(left, right):
        return lax.dot_general(left, right, (((0,), (0,)), ((), ())), preferred_element_type=F32)

    grad_one = outer(back_ref[...], x_ref[...]) * (s_one / strips)
    grad_two = outer(bs_cols[...], first_rows[...]) * (s_two / strips)
    grad_three = outer(second_bf[...], out_ref[...])[:mid] * (s_three / strips)

    def put(ref, parity):
        for k in range(mid // (2 * rows)):
            lo = (2 * k + parity) * rows
            ref[k, :, :c_in] = grad_one[lo : lo + rows]
            for r in range(3):
                for q in range(3):
                    t = 3 * r + q
                    ref[k, :, c_in + t * mid : c_in + (t + 1) * mid] = grad_two[
                        q * mid + lo : q * mid + lo + rows, r * mid : (r + 1) * mid
                    ]
            ref[k, :, c_in + 9 * mid :] = grad_three[lo : lo + rows]

    for own in range(2):

        @pl.when(place_ref[0] % 2 == own)
        def _():
            put(keep_ref, own)
            put(send_ref, 1 - own)


def input_grad_kernel(back_ref, out_ref, params_ref, *rest):
    result_ref = rest[-1]
    c_in = out_ref.shape[1]
    w_first = params_ref[:, :c_in].astype(BF16)
    change = jnp.dot(back_ref[...], w_first, preferred_element_type=F32)
    result_ref[...] = (out_ref[...].astype(F32) + (1.0 / math.sqrt(c_in)) * change).astype(BF16)


def update_kernel(
    place_ref, own_ref, other_ref, own_speed_ref, other_speed_ref, params_ref,
    velocity_ref, weights_ref, *, c_in, mid,
):
    core = place_ref[0] % 2
    pair = place_ref[0] // 2
    halves, rows, width = own_ref.shape
    lane = lax.broadcasted_iota(jnp.int32, (1, 1, width), 2)
    edges = (0, c_in, c_in + 9 * mid, width)

    def column_squares(ref):
        return jnp.sum(jnp.sum(ref[...] ** 2, axis=0, keepdims=True), axis=1, keepdims=True)

    grad_squares = column_squares(own_ref) + column_squares(other_ref)
    param_squares = column_squares(params_ref)
    factor = jnp.zeros((1, 1, width), F32)
    for start, stop in zip(edges[:-1], edges[1:]):
        inside = jnp.logical_and(lane >= start, lane < stop)

        def total(squares):
            return jnp.sum(jnp.where(inside, squares, 0.0), axis=2, keepdims=True)

        trust = jnp.sqrt(total(param_squares)) / (jnp.sqrt(total(grad_squares)) + norm_eps)
        factor = jnp.where(inside, learn_rate * trust, factor)
    factor = factor[0]
    for k in range(halves):
        for parity, grad, speed in ((core, own_ref, own_speed_ref), (1 - core, other_ref, other_speed_ref)):
            tile = 2 * k + parity
            weights_ref[tile] = params_ref[tile] - (momentum * speed[k ^ pair] + factor * grad[k])
    velocity_ref[...] = momentum * own_speed_ref[0] + factor * own_ref[pair]


def full_vmem(count):
    return [pl.BlockSpec(memory_space=pltpu.VMEM) for _ in range(count)]


def in_vmem(*arrays):
    return [pltpu.with_memory_space_constraint(a, pltpu.VMEM) for a in arrays]


def flip(value, axis, bit):
    return lax.ppermute(value, axis, [(i, i ^ bit) for i in range(lax.axis_size(axis))])


def exchange_steps(group, depth):
    across = [(0, 1 << b) for b in range(1, group.bit_length() - 1)]
    along = []
    bit = 1
    while depth % (2 * bit) == 0:
        along.append((1, bit))
        bit *= 2
    steps = []
    for one, two in zip(across, along):
        steps += [(one, two), (two, one)]
    common = min(len(across), len(along))
    steps += [(one, one) for one in across[common:] + along[common:]]
    pairs = []
    for step in steps:
        table = []
        for g in range(group):
            for z in range(depth):
                axis, flipped = step[g % 2]
                to_g, to_z = (g ^ flipped, z) if axis == 0 else (g, z ^ flipped)
                table.append((g * depth + z, to_g * depth + to_z))
        pairs.append(table)
    return pairs, bit


def shards(block_input, mid_first, mid_second, out_grad, params, velocity):
    _, height, width, c_in = block_input.shape
    mid, row = params.shape
    pixels = height * width
    group = lax.axis_size("gx")
    depth = lax.axis_size("gy")
    rows = mid // group
    halves = group // 2
    strips = group * depth
    place = lax.axis_index("gx").reshape(1)
    out_flat = out_grad.reshape(pixels, c_in)
    half = pltpu.VMEM((halves, rows, row), F32)

    keep, send, back_first = pl.pallas_call(
        functools.partial(grad_kernel, height=height, width=width, strips=strips, rows=rows),
        out_shape=(half, half, pltpu.VMEM((pixels, mid), BF16)),
        in_specs=[pl.BlockSpec(memory_space=pltpu.SMEM)] + full_vmem(5),
        out_specs=tuple(full_vmem(3)),
        scratch_shapes=[
            pltpu.VMEM((pixels + 2 * width, 2 * mid), F32),
            pltpu.VMEM((pixels, 2 * mid), F32),
            pltpu.VMEM((pixels + 16, 2 * mid), F32),
            pltpu.VMEM((pixels + 2 * width, 4 * mid), F32),
            pltpu.VMEM((pixels, 4 * mid), BF16),
            pltpu.VMEM((pixels, 4 * mid), BF16),
            pltpu.VMEM((pixels, 2 * mid), BF16),
            pltpu.VMEM((4 * mid, 4 * mid), BF16),
        ],
        name="grads",
    )(
        place,
        block_input.reshape(pixels, c_in),
        mid_first.reshape(height, width * mid),
        mid_second.reshape(height, width * mid),
        out_flat,
        params,
    )

    pieces = 2
    block = pixels // (2 * pieces)

    def input_grad_piece(piece, earlier):
        first = 2 * piece
        operands = [*in_vmem(back_first), out_flat, params] + ([] if earlier is None else [earlier])
        return pl.pallas_call(
            input_grad_kernel,
            out_shape=jax.ShapeDtypeStruct((pixels, c_in), BF16),
            grid=(2,),
            in_specs=[
                pl.BlockSpec((block, mid), lambda i: (first + i, 0)),
                pl.BlockSpec((block, c_in), lambda i: (first + i, 0)),
                pl.BlockSpec((mid, row), lambda i: (0, 0)),
                pl.BlockSpec(memory_space=pl.ANY),
            ][: len(operands)],
            out_specs=pl.BlockSpec((block, c_in), lambda i: (first + i, 0)),
            input_output_aliases={} if earlier is None else {3: 0},
            cost_estimate=pl.CostEstimate(
                flops=2 * pixels * mid * c_in // pieces,
                bytes_accessed=2 * pixels * (2 * c_in + mid) // pieces,
                transcendentals=0,
            ),
            name="input_grad",
        )(*operands)

    total = keep + flip(send, "gx", 1)
    speeds = velocity.reshape(1, rows, row)
    bit = group // 2
    while bit > 1:
        speeds = jnp.stack([speeds, flip(speeds, "gx", bit)], axis=1).reshape(-1, rows, row)
        bit //= 2
    other_speeds = flip(speeds, "gx", 1)
    input_grad = None
    steps, bit = exchange_steps(group, depth)
    for number, table in enumerate(steps):
        total = total + lax.ppermute(total, ("gx", "gy"), table)
        if number in (0, len(steps) - 1):
            input_grad = input_grad_piece(min(number, 1), input_grad)
            total, input_grad = lax.optimization_barrier((total, input_grad))
    turned = [
        lax.ppermute(total, "gy", [(i, (i + turn * bit) % depth) for i in range(depth)])
        for turn in range(1, depth // bit)
    ]
    total = sum(turned, total)
    other = flip(total, "gx", 1)

    new_velocity, next_weights = pl.pallas_call(
        functools.partial(update_kernel, c_in=c_in, mid=mid),
        out_shape=(
            jax.ShapeDtypeStruct((rows, row), F32),
            jax.ShapeDtypeStruct((group, rows, row), F32),
        ),
        in_specs=[pl.BlockSpec(memory_space=pltpu.SMEM)] + full_vmem(5),
        out_specs=tuple(full_vmem(2)),
        name="update",
    )(place, *in_vmem(total, other, speeds, other_speeds, params.reshape(group, rows, row)))
    return (input_grad.reshape(1, height, width, c_in), new_velocity, next_weights.reshape(mid, row))


def solution(mesh):
    return jax.shard_map(
        shards,
        mesh=mesh,
        in_specs=(
            P(("gx", "gy"), None, None, None),
            P(("gx", "gy"), None, None),
            P(("gx", "gy"), None, None),
            P(("gx", "gy"), None, None, None),
            P(),
            P("gx", None),
        ),
        out_specs=(P(("gx", "gy"), None, None, None), P("gx", None), P()),
        check_vma=False,
    )
```

```python
import functools
import math

import jax
import jax.numpy as jnp
from jax import lax
from jax.experimental import pallas as pl
from jax.experimental.pallas import tpu as pltpu
from jax.sharding import PartitionSpec as P

learn_rate = 0.5
momentum = 0.9
norm_eps = 1e-06

F32 = jnp.float32
BF16 = jnp.bfloat16


def divisor_up_to(number, limit):
    return max(d for d in range(1, limit + 1) if number % d == 0)


def spread_pixels(src_ref, dst_ref, base, height, width, mid):
    low = lax.broadcasted_iota(jnp.int32, (height, 2 * mid), 1) < mid
    for pair in range(width // 2):
        slab = src_ref[:, 2 * mid * pair : 2 * mid * (pair + 1)].astype(F32)
        turned = pltpu.roll(slab, mid, 1)
        dst_ref[pl.ds(base + 2 * pair, height, stride=width), :] = jnp.where(low, slab, turned)
        dst_ref[pl.ds(base + 2 * pair + 1, height, stride=width), :] = jnp.where(low, turned, slab)


def grad_kernel(
    place_ref, x_hbm, first_hbm, second_hbm, out_hbm, params_hbm,
    keep_ref, send_ref, back_ref, out_ref,
    x_ref, first_ref, second_ref, params_ref,
    first_px, second_px, bs_px, spread_px, bs_cols, first_rows, second_bf, taps_ref, arrived,
    *, height, width, strips, rows,
):
    moves = [
        pltpu.make_async_copy(source, target, arrived.at[n])
        for n, (source, target) in enumerate(
            (
                (second_hbm, second_ref),
                (first_hbm, first_ref),
                (params_hbm, params_ref),
                (out_hbm, out_ref),
                (x_hbm, x_ref),
            )
        )
    ]
    for move in moves:
        move.start()
    got_second, got_first, got_params, got_out, got_x = moves
    c_in = x_ref.shape[1]
    mid = params_ref.shape[0]
    pixels = height * width
    pad = 8
    s_one, s_two, s_three = (1.0 / math.sqrt(n) for n in (c_in, 9 * mid, mid))
    block_rows = divisor_up_to(height, 8)
    step = block_rows * width
    chunks = [slice(k * step, (k + 1) * step) for k in range(height // block_rows)]
    low = lax.broadcasted_iota(jnp.int32, (step, 2 * mid), 1) < mid
    column = lax.broadcasted_iota(jnp.int32, (step, 2 * mid), 0) % width

    first_px[:width, :] = jnp.zeros((width, 2 * mid), F32)
    first_px[width + pixels :, :] = jnp.zeros((width, 2 * mid), F32)
    spread_px[:width, :] = jnp.zeros((width, 4 * mid), F32)
    spread_px[width + pixels :, :] = jnp.zeros((width, 4 * mid), F32)
    taps_ref[...] = jnp.zeros_like(taps_ref)
    got_second.wait()
    spread_pixels(second_ref, second_px, 0, height, width, mid)
    got_first.wait()
    spread_pixels(first_ref, first_px, width, height, width, mid)
    got_params.wait()
    w_third = params_ref[:, c_in + 9 * mid :].astype(BF16)
    w_third = jnp.concatenate([w_third, w_third], axis=0)
    for r in range(3):
        for q in range(3):
            t = 3 * r + q
            taps_ref[q * mid : (q + 1) * mid, r * mid : (r + 1) * mid] = params_ref[
                :, c_in + t * mid : c_in + (t + 1) * mid
            ].astype(BF16)
    got_out.wait()

    for c in chunks:
        back = lax.dot_general(out_ref[c, :], w_third, (((1,), (1,)), ((), ())), preferred_element_type=F32)
        second = second_px[c, :]
        bs_px[pad + c.start : pad + c.stop, :] = jnp.where(second > 0, back * s_three, 0.0)
        second_bf[c, :] = second.astype(BF16)

    for c in chunks:
        here = bs_px[pad + c.start : pad + c.stop, :]
        after = jnp.where(column < width - 1, bs_px[pad + 1 + c.start : pad + 1 + c.stop, :], 0.0)
        before = jnp.where(column > 0, bs_px[pad - 1 + c.start : pad - 1 + c.stop, :], 0.0)
        cols = jnp.concatenate([jnp.where(low, after, here), before], axis=1).astype(BF16)
        bs_cols[c, :] = cols
        spread_px[width + c.start : width + c.stop, :] = jnp.dot(cols, taps_ref[...], preferred_element_type=F32)
        above = first_px[c, :]
        level = first_px[width + c.start : width + c.stop, :]
        below = first_px[2 * width + c.start : 2 * width + c.stop, :]
        first_rows[c, :] = jnp.concatenate([jnp.where(low, above, level), below], axis=1).astype(BF16)

    for c in chunks:
        top = spread_px[2 * width + c.start : 2 * width + c.stop, : 2 * mid]
        centre = pltpu.roll(spread_px[width + c.start : width + c.stop, : 2 * mid], mid, 1)
        bottom = spread_px[c, 2 * mid :]
        total = (top + centre + bottom) * s_two
        total = jnp.where(first_px[width + c.start : width + c.stop, :] > 0, total, 0.0)
        back_ref[c, :] = total[:, :mid].astype(BF16)

    def outer(left, right):
        return lax.dot_general(left, right, (((0,), (0,)), ((), ())), preferred_element_type=F32)

    grad_two = outer(bs_cols[...], first_rows[...]) * (s_two / strips)
    grad_three = outer(second_bf[...], out_ref[...])[:mid] * (s_three / strips)
    got_x.wait()
    grad_one = outer(back_ref[...], x_ref[...]) * (s_one / strips)

    def put(ref, parity):
        for k in range(mid // (2 * rows)):
            lo = (2 * k + parity) * rows
            ref[k, :, :c_in] = grad_one[lo : lo + rows]
            for r in range(3):
                for q in range(3):
                    t = 3 * r + q
                    ref[k, :, c_in + t * mid : c_in + (t + 1) * mid] = grad_two[
                        q * mid + lo : q * mid + lo + rows, r * mid : (r + 1) * mid
                    ]
            ref[k, :, c_in + 9 * mid :] = grad_three[lo : lo + rows]

    for own in range(2):

        @pl.when(place_ref[0] % 2 == own)
        def _():
            put(keep_ref, own)
            put(send_ref, 1 - own)


def input_grad_kernel(back_ref, out_ref, params_ref, result_ref):
    c_in = out_ref.shape[1]
    w_first = params_ref[:, :c_in].astype(BF16)
    change = jnp.dot(back_ref[...], w_first, preferred_element_type=F32)
    result_ref[...] = (out_ref[...].astype(F32) + (1.0 / math.sqrt(c_in)) * change).astype(BF16)


def update_kernel(
    place_ref, own_ref, other_ref, own_speed_ref, other_speed_ref, params_ref,
    velocity_ref, weights_ref, *, c_in, mid,
):
    core = place_ref[0] % 2
    pair = place_ref[0] // 2
    halves, rows, width = own_ref.shape
    lane = lax.broadcasted_iota(jnp.int32, (1, 1, width), 2)
    edges = (0, c_in, c_in + 9 * mid, width)

    def column_squares(ref):
        return jnp.sum(jnp.sum(ref[...] ** 2, axis=0, keepdims=True), axis=1, keepdims=True)

    grad_squares = column_squares(own_ref) + column_squares(other_ref)
    param_squares = column_squares(params_ref)
    factor = jnp.zeros((1, 1, width), F32)
    for start, stop in zip(edges[:-1], edges[1:]):
        inside = jnp.logical_and(lane >= start, lane < stop)

        def total(squares):
            return jnp.sum(jnp.where(inside, squares, 0.0), axis=2, keepdims=True)

        trust = jnp.sqrt(total(param_squares)) / (jnp.sqrt(total(grad_squares)) + norm_eps)
        factor = jnp.where(inside, learn_rate * trust, factor)
    factor = factor[0]
    for k in range(halves):
        for parity, grad, speed in ((core, own_ref, own_speed_ref), (1 - core, other_ref, other_speed_ref)):
            tile = 2 * k + parity
            weights_ref[tile] = params_ref[tile] - (momentum * speed[k ^ pair] + factor * grad[k])
    velocity_ref[...] = momentum * own_speed_ref[0] + factor * own_ref[pair]


def full_vmem(count):
    return [pl.BlockSpec(memory_space=pltpu.VMEM) for _ in range(count)]


def in_vmem(*arrays):
    return [pltpu.with_memory_space_constraint(a, pltpu.VMEM) for a in arrays]


def flip(value, axis, bit):
    return lax.ppermute(value, axis, [(i, i ^ bit) for i in range(lax.axis_size(axis))])


def exchange_steps(group, depth):
    across = [(0, 1 << b) for b in range(1, group.bit_length() - 1)]
    along = []
    bit = 1
    while depth % (2 * bit) == 0:
        along.append((1, bit))
        bit *= 2
    steps = []
    for one, two in zip(across, along):
        steps += [(one, two), (two, one)]
    common = min(len(across), len(along))
    steps += [(one, one) for one in across[common:] + along[common:]]
    pairs = []
    for step in steps:
        table = []
        for g in range(group):
            for z in range(depth):
                axis, flipped = step[g % 2]
                to_g, to_z = (g ^ flipped, z) if axis == 0 else (g, z ^ flipped)
                table.append((g * depth + z, to_g * depth + to_z))
        pairs.append(table)
    return pairs, bit


def shards(block_input, mid_first, mid_second, out_grad, params, velocity):
    _, height, width, c_in = block_input.shape
    mid, row = params.shape
    pixels = height * width
    group = lax.axis_size("gx")
    depth = lax.axis_size("gy")
    rows = mid // group
    halves = group // 2
    strips = group * depth
    place = lax.axis_index("gx").reshape(1)
    out_flat = out_grad.reshape(pixels, c_in)
    half = pltpu.VMEM((halves, rows, row), F32)

    keep, send, back_first, out_near = pl.pallas_call(
        functools.partial(grad_kernel, height=height, width=width, strips=strips, rows=rows),
        out_shape=(half, half, pltpu.VMEM((pixels, mid), BF16), pltpu.VMEM((pixels, c_in), BF16)),
        in_specs=[pl.BlockSpec(memory_space=pltpu.SMEM)] + [pl.BlockSpec(memory_space=pltpu.HBM)] * 5,
        out_specs=tuple(full_vmem(4)),
        scratch_shapes=[
            pltpu.VMEM((pixels, c_in), BF16),
            pltpu.VMEM((height, width * mid), BF16),
            pltpu.VMEM((height, width * mid), BF16),
            pltpu.VMEM((mid, row), F32),
            pltpu.VMEM((pixels + 2 * width, 2 * mid), F32),
            pltpu.VMEM((pixels, 2 * mid), F32),
            pltpu.VMEM((pixels + 16, 2 * mid), F32),
            pltpu.VMEM((pixels + 2 * width, 4 * mid), F32),
            pltpu.VMEM((pixels, 4 * mid), BF16),
            pltpu.VMEM((pixels, 4 * mid), BF16),
            pltpu.VMEM((pixels, 2 * mid), BF16),
            pltpu.VMEM((4 * mid, 4 * mid), BF16),
            pltpu.SemaphoreType.DMA((5,)),
        ],
        name="grads",
    )(
        place,
        block_input.reshape(pixels, c_in),
        mid_first.reshape(height, width * mid),
        mid_second.reshape(height, width * mid),
        out_flat,
        params,
    )

    input_grad = pl.pallas_call(
        input_grad_kernel,
        out_shape=pltpu.VMEM((pixels, c_in), BF16),
        in_specs=full_vmem(3),
        out_specs=full_vmem(1)[0],
        cost_estimate=pl.CostEstimate(
            flops=2 * pixels * mid * c_in, bytes_accessed=2 * pixels * (2 * c_in + mid), transcendentals=0
        ),
        name="input_grad",
    )(*in_vmem(back_first, out_near, params))

    total = keep + flip(send, "gx", 1)
    speeds = velocity.reshape(1, rows, row)
    bit = group // 2
    while bit > 1:
        speeds = jnp.stack([speeds, flip(speeds, "gx", bit)], axis=1).reshape(-1, rows, row)
        bit //= 2
    other_speeds = flip(speeds, "gx", 1)
    steps, bit = exchange_steps(group, depth)
    for number, table in enumerate(steps):
        total = total + lax.ppermute(total, ("gx", "gy"), table)
        if number == 0:
            total, input_grad = lax.optimization_barrier((total, input_grad))
    turned = [
        lax.ppermute(total, "gy", [(i, (i + turn * bit) % depth) for i in range(depth)])
        for turn in range(1, depth // bit)
    ]
    total = sum(turned, total)
    other = flip(total, "gx", 1)

    new_velocity, next_weights = pl.pallas_call(
        functools.partial(update_kernel, c_in=c_in, mid=mid),
        out_shape=(
            jax.ShapeDtypeStruct((rows, row), F32),
            jax.ShapeDtypeStruct((group, rows, row), F32),
        ),
        in_specs=[pl.BlockSpec(memory_space=pltpu.SMEM)] + full_vmem(5),
        out_specs=tuple(full_vmem(2)),
        name="update",
    )(place, *in_vmem(total, other, speeds, other_speeds, params.reshape(group, rows, row)))
    return (input_grad.reshape(1, height, width, c_in), new_velocity, next_weights.reshape(mid, row))


def solution(mesh):
    return jax.shard_map(
        shards,
        mesh=mesh,
        in_specs=(
            P(("gx", "gy"), None, None, None),
            P(("gx", "gy"), None, None),
            P(("gx", "gy"), None, None),
            P(("gx", "gy"), None, None, None),
            P(),
            P("gx", None),
        ),
        out_specs=(P(("gx", "gy"), None, None, None), P("gx", None), P()),
        check_vma=False,
    )
```

```python
import functools
import math

import jax
import jax.numpy as jnp
from jax import lax
from jax.experimental import pallas as pl
from jax.experimental.pallas import tpu as pltpu
from jax.sharding import PartitionSpec as P

learn_rate = 0.5
momentum = 0.9
norm_eps = 1e-06

F32 = jnp.float32
BF16 = jnp.bfloat16


def divisor_up_to(number, limit):
    return max(d for d in range(1, limit + 1) if number % d == 0)


def round_up(number, multiple):
    return -(-number // multiple) * multiple


def grad_kernel(
    place_ref, x_hbm, first_hbm, second_hbm, out_hbm, params_hbm,
    keep_ref, send_ref, back_ref, out_ref,
    x_ref, first_ref, second_ref, params_ref,
    bs_cols, first_rows, second_bf, taps_ref, arrived, *blocks,
    height, width, strips, rows,
):
    count = len(blocks) // 4
    second_px, first_px, bs_px, spread_px = (blocks[n * count : (n + 1) * count] for n in range(4))
    moves = [
        pltpu.make_async_copy(source, target, arrived.at[n])
        for n, (source, target) in enumerate(
            (
                (second_hbm, second_ref),
                (first_hbm, first_ref),
                (params_hbm, params_ref),
                (out_hbm, out_ref),
                (x_hbm, x_ref),
            )
        )
    ]
    for move in moves:
        move.start()
    got_second, got_first, got_params, got_out, got_x = moves
    c_in = x_ref.shape[1]
    mid = params_ref.shape[0]
    pixels = height * width
    pad = 8
    s_one, s_two, s_three = (1.0 / math.sqrt(n) for n in (c_in, 9 * mid, mid))
    block_rows = divisor_up_to(height, 8)
    step = block_rows * width
    chunks = [slice(k * step, (k + 1) * step) for k in range(height // block_rows)]
    low = lax.broadcasted_iota(jnp.int32, (step, 2 * mid), 1) < mid
    low_slab = lax.broadcasted_iota(jnp.int32, (block_rows, 2 * mid), 1) < mid
    column = lax.broadcasted_iota(jnp.int32, (step, 2 * mid), 0) % width

    taps_ref[...] = jnp.zeros_like(taps_ref)
    got_second.wait()
    got_first.wait()

    def to_pixels(number):
        for ref, px in ((second_ref, second_px[number]), (first_ref, first_px[number])):
            for k in range(width // 2):
                slab = ref[
                    number * block_rows : (number + 1) * block_rows, 2 * mid * k : 2 * mid * (k + 1)
                ].astype(F32)
                turned = pltpu.roll(slab, mid, 1)
                px[pl.ds(2 * k, block_rows, stride=width), :] = jnp.where(low_slab, slab, turned)
                px[pl.ds(2 * k + 1, block_rows, stride=width), :] = jnp.where(low_slab, turned, slab)

    def enter(number):
        c = chunks[number]
        second = second_px[number][...]
        second_bf[c, :] = second[:, :mid].astype(BF16)
        back = lax.dot_general(out_ref[c, :], w_third, (((1,), (1,)), ((), ())), preferred_element_type=F32)
        here = jnp.where(second > 0, back * s_three, 0.0)
        px = bs_px[number]
        px[pad : pad + step, :] = here
        after = jnp.where(column < width - 1, px[pad + 1 : pad + 1 + step, :], 0.0)
        before = jnp.where(column > 0, px[pad - 1 : pad - 1 + step, :], 0.0)
        cols = jnp.concatenate([jnp.where(low, after, here), before], axis=1).astype(BF16)
        bs_cols[c, :] = cols
        spread_px[number][...] = jnp.dot(cols, taps_ref[...], preferred_element_type=F32)

    def row_above(blocks, number, lanes):
        head = blocks[number - 1][step - width :, lanes] if number else jnp.zeros((width, 2 * mid), F32)
        return jnp.concatenate([head, blocks[number][: step - width, lanes]], axis=0)

    def row_below(blocks, number, lanes):
        last = number + 1 == len(chunks)
        tail = jnp.zeros((width, 2 * mid), F32) if last else blocks[number + 1][:width, lanes]
        return jnp.concatenate([blocks[number][width:, lanes], tail], axis=0)

    def leave(number):
        c = chunks[number]
        front, rear = slice(0, 2 * mid), slice(2 * mid, 4 * mid)
        level = first_px[number][...]
        above = row_above(first_px, number, front)
        below = row_below(first_px, number, front)
        first_rows[c, :] = jnp.concatenate([jnp.where(low, above, level), below], axis=1).astype(BF16)
        top = row_below(spread_px, number, front)
        centre = pltpu.roll(spread_px[number][:, front], mid, 1)
        bottom = row_above(spread_px, number, rear)
        total = jnp.where(level > 0, (top + centre + bottom) * s_two, 0.0)
        back_ref[c, :] = total[:, :mid].astype(BF16)

    for number in range(len(chunks)):
        to_pixels(number)
    got_out.wait()
    got_x.wait()
    got_params.wait()
    w_third = params_ref[:, c_in + 9 * mid :].astype(BF16)
    w_third = jnp.concatenate([w_third, w_third], axis=0)
    for r in range(3):
        for q in range(3):
            t = 3 * r + q
            taps_ref[q * mid : (q + 1) * mid, r * mid : (r + 1) * mid] = params_ref[
                :, c_in + t * mid : c_in + (t + 1) * mid
            ].astype(BF16)
    for number in range(len(chunks)):
        enter(number)
        if number:
            leave(number - 1)
    leave(len(chunks) - 1)

    spans = [slice(0, pixels)]

    def outer(left, wide, right):
        terms = [
            lax.dot_general(left[k, :wide], right[k, :], (((0,), (0,)), ((), ())), preferred_element_type=F32)
            for k in spans
        ]
        return sum(terms[1:], terms[0])

    even = place_ref[0] % 2 == 0

    def put(grad, column):
        columns = slice(column, column + grad.shape[1])
        for k in range(mid // (2 * rows)):
            lo = 2 * k * rows
            one, two = grad[lo : lo + rows], grad[lo + rows : lo + 2 * rows]
            keep_ref[k, :, columns] = jnp.where(even, one, two)
            send_ref[k, :, columns] = jnp.where(even, two, one)

    put(outer(second_bf, mid, out_ref) * (s_three / strips), c_in + 9 * mid)
    grad_two = outer(bs_cols, 3 * mid, first_rows) * (s_two / strips)
    for r in range(3):
        for q in range(3):
            put(grad_two[q * mid : (q + 1) * mid, r * mid : (r + 1) * mid], c_in + (3 * r + q) * mid)
    put(outer(back_ref, mid, x_ref) * (s_one / strips), 0)


def input_grad_kernel(back_ref, out_ref, params_ref, result_ref):
    c_in = out_ref.shape[1]
    w_first = params_ref[:, :c_in].astype(BF16)
    change = jnp.dot(back_ref[...], w_first, preferred_element_type=F32)
    result_ref[...] = (out_ref[...].astype(F32) + (1.0 / math.sqrt(c_in)) * change).astype(BF16)


def update_kernel(
    place_ref, own_ref, other_ref, own_speed_ref, other_speed_ref, params_ref,
    velocity_ref, weights_ref, *, c_in, mid,
):
    core = place_ref[0] % 2
    pair = place_ref[0] // 2
    halves, rows, width = own_ref.shape
    lane = lax.broadcasted_iota(jnp.int32, (1, 1, width), 2)
    edges = (0, c_in, c_in + 9 * mid, width)

    def column_squares(ref):
        return jnp.sum(jnp.sum(ref[...] ** 2, axis=0, keepdims=True), axis=1, keepdims=True)

    grad_squares = column_squares(own_ref) + column_squares(other_ref)
    param_squares = column_squares(params_ref)
    factor = jnp.zeros((1, 1, width), F32)
    for start, stop in zip(edges[:-1], edges[1:]):
        inside = jnp.logical_and(lane >= start, lane < stop)

        def total(squares):
            return jnp.sum(jnp.where(inside, squares, 0.0), axis=2, keepdims=True)

        trust = jnp.sqrt(total(param_squares)) / (jnp.sqrt(total(grad_squares)) + norm_eps)
        factor = jnp.where(inside, learn_rate * trust, factor)
    factor = factor[0]
    for k in range(halves):
        for parity, grad, speed in ((core, own_ref, own_speed_ref), (1 - core, other_ref, other_speed_ref)):
            tile = 2 * k + parity
            weights_ref[tile] = params_ref[tile] - (momentum * speed[k ^ pair] + factor * grad[k])
    velocity_ref[...] = momentum * own_speed_ref[0] + factor * own_ref[pair]


def full_vmem(count):
    return [pl.BlockSpec(memory_space=pltpu.VMEM) for _ in range(count)]


def in_vmem(*arrays):
    return [pltpu.with_memory_space_constraint(a, pltpu.VMEM) for a in arrays]


def flip(value, axis, bit):
    return lax.ppermute(value, axis, [(i, i ^ bit) for i in range(lax.axis_size(axis))])


def exchange_steps(group, depth):
    across = [(0, 1 << b) for b in range(1, group.bit_length() - 1)]
    along = []
    bit = 1
    while depth % (2 * bit) == 0:
        along.append((1, bit))
        bit *= 2
    steps = []
    for one, two in zip(across, along):
        steps += [(one, two), (two, one)]
    common = min(len(across), len(along))
    steps += [(one, one) for one in across[common:] + along[common:]]
    pairs = []
    for step in steps:
        table = []
        for g in range(group):
            for z in range(depth):
                axis, flipped = step[g % 2]
                to_g, to_z = (g ^ flipped, z) if axis == 0 else (g, z ^ flipped)
                table.append((g * depth + z, to_g * depth + to_z))
        pairs.append(table)
    return pairs, bit


def shards(block_input, mid_first, mid_second, out_grad, params, velocity):
    _, height, width, c_in = block_input.shape
    mid, row = params.shape
    pixels = height * width
    group = lax.axis_size("gx")
    depth = lax.axis_size("gy")
    rows = mid // group
    halves = group // 2
    strips = group * depth
    place = lax.axis_index("gx").reshape(1)
    out_flat = out_grad.reshape(pixels, c_in)
    step = divisor_up_to(height, 8) * width
    half = pltpu.VMEM((halves, rows, row), F32)

    keep, send, back_first, out_near = pl.pallas_call(
        functools.partial(grad_kernel, height=height, width=width, strips=strips, rows=rows),
        out_shape=(half, half, pltpu.VMEM((pixels, mid), BF16), pltpu.VMEM((pixels, c_in), BF16)),
        in_specs=[pl.BlockSpec(memory_space=pltpu.SMEM)] + [pl.BlockSpec(memory_space=pltpu.HBM)] * 5,
        out_specs=tuple(full_vmem(4)),
        scratch_shapes=[
            pltpu.VMEM((pixels, c_in), BF16),
            pltpu.VMEM((height, width * mid), BF16),
            pltpu.VMEM((height, width * mid), BF16),
            pltpu.VMEM((mid, row), F32),
            pltpu.VMEM((pixels, 4 * mid), BF16),
            pltpu.VMEM((pixels, 4 * mid), BF16),
            pltpu.VMEM((pixels, mid), BF16),
            pltpu.VMEM((4 * mid, 4 * mid), BF16),
            pltpu.SemaphoreType.DMA((5,)),
        ]
        + [
            pltpu.VMEM(shape, F32)
            for shape in ((step, 2 * mid), (step, 2 * mid), (step + 16, 2 * mid), (step, 4 * mid))
            for _ in range(pixels // step)
        ],
        name="grads",
    )(
        place,
        block_input.reshape(pixels, c_in),
        mid_first.reshape(height, width * mid),
        mid_second.reshape(height, width * mid),
        out_flat,
        params,
    )

    input_grad = pl.pallas_call(
        input_grad_kernel,
        out_shape=pltpu.VMEM((pixels, c_in), BF16),
        in_specs=full_vmem(3),
        out_specs=full_vmem(1)[0],
        cost_estimate=pl.CostEstimate(
            flops=2 * pixels * mid * c_in, bytes_accessed=2 * pixels * (2 * c_in + mid), transcendentals=0
        ),
        name="input_grad",
    )(*in_vmem(back_first, out_near, params))

    total = keep + flip(send, "gx", 1)
    speeds = velocity.reshape(1, rows, row)
    bit = group // 2
    while bit > 1:
        speeds = jnp.stack([speeds, flip(speeds, "gx", bit)], axis=1).reshape(-1, rows, row)
        bit //= 2
    other_speeds = flip(speeds, "gx", 1)
    steps, bit = exchange_steps(group, depth)
    for number, table in enumerate(steps):
        total = total + lax.ppermute(total, ("gx", "gy"), table)
        if number == 0:
            total, input_grad = lax.optimization_barrier((total, input_grad))
    turned = [
        lax.ppermute(total, "gy", [(i, (i + turn * bit) % depth) for i in range(depth)])
        for turn in range(1, depth // bit)
    ]
    total = sum(turned, total)
    other = flip(total, "gx", 1)

    new_velocity, next_weights = pl.pallas_call(
        functools.partial(update_kernel, c_in=c_in, mid=mid),
        out_shape=(
            jax.ShapeDtypeStruct((rows, row), F32),
            jax.ShapeDtypeStruct((group, rows, row), F32),
        ),
        in_specs=[pl.BlockSpec(memory_space=pltpu.SMEM)] + full_vmem(5),
        out_specs=tuple(full_vmem(2)),
        name="update",
    )(place, *in_vmem(total, other, speeds, other_speeds, params.reshape(group, rows, row)))
    return (input_grad.reshape(1, height, width, c_in), new_velocity, next_weights.reshape(mid, row))


def solution(mesh):
    return jax.shard_map(
        shards,
        mesh=mesh,
        in_specs=(
            P(("gx", "gy"), None, None, None),
            P(("gx", "gy"), None, None),
            P(("gx", "gy"), None, None),
            P(("gx", "gy"), None, None, None),
            P(),
            P("gx", None),
        ),
        out_specs=(P(("gx", "gy"), None, None, None), P("gx", None), P()),
        check_vma=False,
    )
```

```python
import functools
import math

import jax
import jax.numpy as jnp
from jax import lax
from jax.experimental import pallas as pl
from jax.experimental.pallas import tpu as pltpu
from jax.sharding import PartitionSpec as P

learn_rate = 0.5
momentum = 0.9
norm_eps = 1e-06

F32 = jnp.float32
BF16 = jnp.bfloat16


def divisor_up_to(number, limit):
    return max(d for d in range(1, limit + 1) if number % d == 0)


def round_up(number, multiple):
    return -(-number // multiple) * multiple


def grad_kernel(
    place_ref, x_hbm, first_hbm, second_hbm, out_hbm, params_hbm,
    back_ref, out_ref, *rest, height, width, strips, rows, streams,
):
    keep_refs, send_refs, rest = rest[:streams], rest[streams : 2 * streams], rest[2 * streams :]
    x_ref, first_ref, second_ref, params_ref, bs_cols, first_rows, second_bf, taps_ref, arrived, *blocks = rest
    count = len(blocks) // 4
    second_px, first_px, bs_px, spread_px = (blocks[n * count : (n + 1) * count] for n in range(4))
    moves = [
        pltpu.make_async_copy(source, target, arrived.at[n])
        for n, (source, target) in enumerate(
            (
                (second_hbm, second_ref),
                (first_hbm, first_ref),
                (params_hbm, params_ref),
                (out_hbm, out_ref),
                (x_hbm, x_ref),
            )
        )
    ]
    for move in moves:
        move.start()
    got_second, got_first, got_params, got_out, got_x = moves
    c_in = x_ref.shape[1]
    mid = params_ref.shape[0]
    pixels = height * width
    pad = 8
    s_one, s_two, s_three = (1.0 / math.sqrt(n) for n in (c_in, 9 * mid, mid))
    block_rows = divisor_up_to(height, 8)
    step = block_rows * width
    chunks = [slice(k * step, (k + 1) * step) for k in range(height // block_rows)]
    low = lax.broadcasted_iota(jnp.int32, (step, 2 * mid), 1) < mid
    low_slab = lax.broadcasted_iota(jnp.int32, (block_rows, 2 * mid), 1) < mid
    column = lax.broadcasted_iota(jnp.int32, (step, 2 * mid), 0) % width

    taps_ref[...] = jnp.zeros_like(taps_ref)
    got_second.wait()
    got_first.wait()

    def to_pixels(number):
        for ref, px in ((second_ref, second_px[number]), (first_ref, first_px[number])):
            for k in range(width // 2):
                slab = ref[
                    number * block_rows : (number + 1) * block_rows, 2 * mid * k : 2 * mid * (k + 1)
                ].astype(F32)
                turned = pltpu.roll(slab, mid, 1)
                px[pl.ds(2 * k, block_rows, stride=width), :] = jnp.where(low_slab, slab, turned)
                px[pl.ds(2 * k + 1, block_rows, stride=width), :] = jnp.where(low_slab, turned, slab)

    def enter(number):
        c = chunks[number]
        second = second_px[number][...]
        second_bf[c, :] = second[:, :mid].astype(BF16)
        back = lax.dot_general(out_ref[c, :], w_third, (((1,), (1,)), ((), ())), preferred_element_type=F32)
        here = jnp.where(second > 0, back * s_three, 0.0)
        px = bs_px[number]
        px[pad : pad + step, :] = here
        after = jnp.where(column < width - 1, px[pad + 1 : pad + 1 + step, :], 0.0)
        before = jnp.where(column > 0, px[pad - 1 : pad - 1 + step, :], 0.0)
        cols = jnp.concatenate([jnp.where(low, after, here), before], axis=1).astype(BF16)
        bs_cols[c, :] = cols
        spread_px[number][...] = jnp.dot(cols, taps_ref[...], preferred_element_type=F32)

    def row_above(blocks, number, lanes):
        head = blocks[number - 1][step - width :, lanes] if number else jnp.zeros((width, 2 * mid), F32)
        return jnp.concatenate([head, blocks[number][: step - width, lanes]], axis=0)

    def row_below(blocks, number, lanes):
        last = number + 1 == len(chunks)
        tail = jnp.zeros((width, 2 * mid), F32) if last else blocks[number + 1][:width, lanes]
        return jnp.concatenate([blocks[number][width:, lanes], tail], axis=0)

    def leave(number):
        c = chunks[number]
        front, rear = slice(0, 2 * mid), slice(2 * mid, 4 * mid)
        level = first_px[number][...]
        above = row_above(first_px, number, front)
        below = row_below(first_px, number, front)
        first_rows[c, :] = jnp.concatenate([jnp.where(low, above, level), below], axis=1).astype(BF16)
        top = row_below(spread_px, number, front)
        centre = pltpu.roll(spread_px[number][:, front], mid, 1)
        bottom = row_above(spread_px, number, rear)
        total = jnp.where(level > 0, (top + centre + bottom) * s_two, 0.0)
        back_ref[c, :] = total[:, :mid].astype(BF16)

    for number in range(len(chunks)):
        to_pixels(number)
    got_out.wait()
    got_x.wait()
    got_params.wait()
    w_third = params_ref[:, c_in + 9 * mid :].astype(BF16)
    w_third = jnp.concatenate([w_third, w_third], axis=0)
    for r in range(3):
        for q in range(3):
            t = 3 * r + q
            taps_ref[q * mid : (q + 1) * mid, r * mid : (r + 1) * mid] = params_ref[
                :, c_in + t * mid : c_in + (t + 1) * mid
            ].astype(BF16)
    for number in range(len(chunks)):
        enter(number)
        if number:
            leave(number - 1)
    leave(len(chunks) - 1)

    spans = [slice(0, pixels)]

    def outer(left, wide, right):
        terms = [
            lax.dot_general(left[k, :wide], right[k, :], (((0,), (0,)), ((), ())), preferred_element_type=F32)
            for k in spans
        ]
        return sum(terms[1:], terms[0])

    even = place_ref[0] % 2 == 0

    def put(grad, column):
        columns = slice(column, column + grad.shape[1])
        for k in range(mid // (2 * rows)):
            lo = 2 * k * rows
            one, two = grad[lo : lo + rows], grad[lo + rows : lo + 2 * rows]
            stream, tile = divmod(k, keep_refs[0].shape[0])
            keep_refs[stream][tile, :, columns] = jnp.where(even, one, two)
            send_refs[stream][tile, :, columns] = jnp.where(even, two, one)

    put(outer(second_bf, mid, out_ref) * (s_three / strips), c_in + 9 * mid)
    grad_two = outer(bs_cols, 3 * mid, first_rows) * (s_two / strips)
    for r in range(3):
        for q in range(3):
            put(grad_two[q * mid : (q + 1) * mid, r * mid : (r + 1) * mid], c_in + (3 * r + q) * mid)
    put(outer(back_ref, mid, x_ref) * (s_one / strips), 0)


def input_grad_kernel(back_ref, out_ref, params_ref, result_ref):
    c_in = out_ref.shape[1]
    w_first = params_ref[:, :c_in].astype(BF16)
    change = jnp.dot(back_ref[...], w_first, preferred_element_type=F32)
    result_ref[...] = (out_ref[...].astype(F32) + (1.0 / math.sqrt(c_in)) * change).astype(BF16)


def update_kernel(
    place_ref, own_speed_ref, other_speed_ref, params_ref, *rest, c_in, mid,
):
    *grads, velocity_ref, weights_ref = rest
    streams = len(grads) // 2
    own_refs, other_refs = grads[:streams], grads[streams:]
    core = place_ref[0] % 2
    pair = place_ref[0] // 2
    tiles, rows, width = own_refs[0].shape
    lane = lax.broadcasted_iota(jnp.int32, (1, 1, width), 2)
    edges = (0, c_in, c_in + 9 * mid, width)

    def column_squares(ref):
        return jnp.sum(jnp.sum(ref[...] ** 2, axis=0, keepdims=True), axis=1, keepdims=True)

    grad_squares = sum(column_squares(ref) for ref in grads)
    param_squares = column_squares(params_ref)
    factor = jnp.zeros((1, 1, width), F32)
    for start, stop in zip(edges[:-1], edges[1:]):
        inside = jnp.logical_and(lane >= start, lane < stop)

        def total(squares):
            return jnp.sum(jnp.where(inside, squares, 0.0), axis=2, keepdims=True)

        trust = jnp.sqrt(total(param_squares)) / (jnp.sqrt(total(grad_squares)) + norm_eps)
        factor = jnp.where(inside, learn_rate * trust, factor)
    factor = factor[0]
    for k in range(tiles * streams):
        for parity, refs, speed in ((core, own_refs, own_speed_ref), (1 - core, other_refs, other_speed_ref)):
            tile = 2 * k + parity
            grad = refs[k // tiles][k % tiles]
            weights_ref[tile] = params_ref[tile] - (momentum * speed[k ^ pair] + factor * grad)
    mine = own_refs[0][pair % tiles]
    for number in range(1, streams):
        mine = jnp.where(pair // tiles == number, own_refs[number][pair % tiles], mine)
    velocity_ref[...] = momentum * own_speed_ref[0] + factor * mine


def full_vmem(count):
    return [pl.BlockSpec(memory_space=pltpu.VMEM) for _ in range(count)]


def in_vmem(*arrays):
    return [pltpu.with_memory_space_constraint(a, pltpu.VMEM) for a in arrays]


def flip(value, axis, bit):
    return lax.ppermute(value, axis, [(i, i ^ bit) for i in range(lax.axis_size(axis))])


def exchange_steps(group, depth):
    across = [(0, 1 << b) for b in range(1, group.bit_length() - 1)]
    along = []
    bit = 1
    while depth % (2 * bit) == 0:
        along.append((1, bit))
        bit *= 2
    steps = []
    for one, two in zip(across, along):
        steps += [(one, two), (two, one)]
    common = min(len(across), len(along))
    steps += [(one, one) for one in across[common:] + along[common:]]
    pairs = []
    for step in steps:
        table = []
        for g in range(group):
            for z in range(depth):
                axis, flipped = step[g % 2]
                to_g, to_z = (g ^ flipped, z) if axis == 0 else (g, z ^ flipped)
                table.append((g * depth + z, to_g * depth + to_z))
        pairs.append(table)
    return pairs, bit


def shards(block_input, mid_first, mid_second, out_grad, params, velocity):
    _, height, width, c_in = block_input.shape
    mid, row = params.shape
    pixels = height * width
    group = lax.axis_size("gx")
    depth = lax.axis_size("gy")
    rows = mid // group
    halves = group // 2
    strips = group * depth
    place = lax.axis_index("gx").reshape(1)
    out_flat = out_grad.reshape(pixels, c_in)
    step = divisor_up_to(height, 8) * width
    streams = 2 if halves % 2 == 0 else 1
    part = pltpu.VMEM((halves // streams, rows, row), F32)

    back_first, out_near, *parts = pl.pallas_call(
        functools.partial(grad_kernel, height=height, width=width, strips=strips, rows=rows, streams=streams),
        out_shape=(pltpu.VMEM((pixels, mid), BF16), pltpu.VMEM((pixels, c_in), BF16), *[part] * (2 * streams)),
        in_specs=[pl.BlockSpec(memory_space=pltpu.SMEM)] + [pl.BlockSpec(memory_space=pltpu.HBM)] * 5,
        out_specs=tuple(full_vmem(2 + 2 * streams)),
        scratch_shapes=[
            pltpu.VMEM((pixels, c_in), BF16),
            pltpu.VMEM((height, width * mid), BF16),
            pltpu.VMEM((height, width * mid), BF16),
            pltpu.VMEM((mid, row), F32),
            pltpu.VMEM((pixels, 4 * mid), BF16),
            pltpu.VMEM((pixels, 4 * mid), BF16),
            pltpu.VMEM((pixels, mid), BF16),
            pltpu.VMEM((4 * mid, 4 * mid), BF16),
            pltpu.SemaphoreType.DMA((5,)),
        ]
        + [
            pltpu.VMEM(shape, F32)
            for shape in ((step, 2 * mid), (step, 2 * mid), (step + 16, 2 * mid), (step, 4 * mid))
            for _ in range(pixels // step)
        ],
        name="grads",
    )(
        place,
        block_input.reshape(pixels, c_in),
        mid_first.reshape(height, width * mid),
        mid_second.reshape(height, width * mid),
        out_flat,
        params,
    )

    input_grad = pl.pallas_call(
        input_grad_kernel,
        out_shape=pltpu.VMEM((pixels, c_in), BF16),
        in_specs=full_vmem(3),
        out_specs=full_vmem(1)[0],
        cost_estimate=pl.CostEstimate(
            flops=2 * pixels * mid * c_in, bytes_accessed=2 * pixels * (2 * c_in + mid), transcendentals=0
        ),
        name="input_grad",
    )(*in_vmem(back_first, out_near, params))

    totals = [keep + flip(send, "gx", 1) for keep, send in zip(parts[:streams], parts[streams:])]
    speeds = velocity.reshape(1, rows, row)
    bit = group // 2
    while bit > 1:
        speeds = jnp.stack([speeds, flip(speeds, "gx", bit)], axis=1).reshape(-1, rows, row)
        bit //= 2
    other_speeds = flip(speeds, "gx", 1)
    steps, bit = exchange_steps(group, depth)
    for number, table in enumerate(steps):
        totals = [total + lax.ppermute(total, ("gx", "gy"), table) for total in totals]
        if number == 0:
            totals[0], input_grad = lax.optimization_barrier((totals[0], input_grad))
    for turn in range(1, depth // bit):
        table = [(i, (i + turn * bit) % depth) for i in range(depth)]
        terms = [lax.ppermute(total, "gy", table) for total in totals]
        sums = terms if turn == 1 else [a + b for a, b in zip(sums, terms)]
    if depth > bit:
        totals = [a + b for a, b in zip(totals, sums)]
    others = [flip(total, "gx", 1) for total in totals]

    new_velocity, next_weights = pl.pallas_call(
        functools.partial(update_kernel, c_in=c_in, mid=mid),
        out_shape=(
            jax.ShapeDtypeStruct((rows, row), F32),
            jax.ShapeDtypeStruct((group, rows, row), F32),
        ),
        in_specs=[pl.BlockSpec(memory_space=pltpu.SMEM)] + full_vmem(3 + 2 * streams),
        out_specs=tuple(full_vmem(2)),
        name="update",
    )(place, *in_vmem(speeds, other_speeds, params.reshape(group, rows, row), *totals, *others))
    return (input_grad.reshape(1, height, width, c_in), new_velocity, next_weights.reshape(mid, row))


def solution(mesh):
    return jax.shard_map(
        shards,
        mesh=mesh,
        in_specs=(
            P(("gx", "gy"), None, None, None),
            P(("gx", "gy"), None, None),
            P(("gx", "gy"), None, None),
            P(("gx", "gy"), None, None, None),
            P(),
            P("gx", None),
        ),
        out_specs=(P(("gx", "gy"), None, None, None), P("gx", None), P()),
        check_vma=False,
    )
```

```python
import functools
import math

import jax
import jax.numpy as jnp
from jax import lax
from jax.experimental import pallas as pl
from jax.experimental.pallas import tpu as pltpu
from jax.sharding import PartitionSpec as P

learn_rate = 0.5
momentum = 0.9
norm_eps = 1e-06

F32 = jnp.float32
BF16 = jnp.bfloat16


def divisor_up_to(number, limit):
    return max(d for d in range(1, limit + 1) if number % d == 0)


def round_up(number, multiple):
    return -(-number // multiple) * multiple


def grad_kernel(
    place_ref, x_hbm, first_hbm, second_hbm, out_hbm, params_hbm,
    back_ref, out_ref, *rest, height, width, strips, rows, streams,
):
    keep_refs, send_refs, rest = rest[:streams], rest[streams : 2 * streams], rest[2 * streams :]
    x_ref, first_ref, second_ref, params_ref, bs_cols, first_rows, second_bf, taps_ref, arrived, *blocks = rest
    count = len(blocks) // 4
    second_px, first_px, bs_px, spread_px = (blocks[n * count : (n + 1) * count] for n in range(4))
    moves = [
        pltpu.make_async_copy(source, target, arrived.at[n])
        for n, (source, target) in enumerate(
            (
                (second_hbm, second_ref),
                (first_hbm, first_ref),
                (params_hbm, params_ref),
                (out_hbm, out_ref),
                (x_hbm, x_ref),
            )
        )
    ]
    for move in moves:
        move.start()
    got_second, got_first, got_params, got_out, got_x = moves
    c_in = x_ref.shape[1]
    mid = params_ref.shape[0]
    pixels = height * width
    pad = 8
    s_one, s_two, s_three = (1.0 / math.sqrt(n) for n in (c_in, 9 * mid, mid))
    block_rows = divisor_up_to(height, 8)
    step = block_rows * width
    chunks = [slice(k * step, (k + 1) * step) for k in range(height // block_rows)]
    low = lax.broadcasted_iota(jnp.int32, (step, 2 * mid), 1) < mid
    low_slab = lax.broadcasted_iota(jnp.int32, (block_rows, 2 * mid), 1) < mid
    column = lax.broadcasted_iota(jnp.int32, (step, 2 * mid), 0) % width

    taps_ref[...] = jnp.zeros_like(taps_ref)
    got_second.wait()
    got_first.wait()

    def to_pixels(number):
        for ref, px in ((second_ref, second_px[number]), (first_ref, first_px[number])):
            for k in range(width // 2):
                slab = ref[
                    number * block_rows : (number + 1) * block_rows, 2 * mid * k : 2 * mid * (k + 1)
                ].astype(F32)
                turned = pltpu.roll(slab, mid, 1)
                px[pl.ds(2 * k, block_rows, stride=width), :] = jnp.where(low_slab, slab, turned)
                px[pl.ds(2 * k + 1, block_rows, stride=width), :] = jnp.where(low_slab, turned, slab)

    def enter(number):
        c = chunks[number]
        second = second_px[number][...]
        second_bf[c, :] = second[:, :mid].astype(BF16)
        back = lax.dot_general(out_ref[c, :], w_third, (((1,), (1,)), ((), ())), preferred_element_type=F32)
        here = jnp.where(second > 0, back * s_three, 0.0)
        px = bs_px[number]
        px[pad : pad + step, :] = here
        after = jnp.where(column < width - 1, px[pad + 1 : pad + 1 + step, :], 0.0)
        before = jnp.where(column > 0, px[pad - 1 : pad - 1 + step, :], 0.0)
        cols = jnp.concatenate([jnp.where(low, after, here), before], axis=1).astype(BF16)
        bs_cols[c, :] = cols
        spread_px[number][...] = jnp.dot(cols, taps_ref[...], preferred_element_type=F32)

    def row_above(blocks, number, lanes):
        head = blocks[number - 1][step - width :, lanes] if number else jnp.zeros((width, 2 * mid), F32)
        return jnp.concatenate([head, blocks[number][: step - width, lanes]], axis=0)

    def row_below(blocks, number, lanes):
        last = number + 1 == len(chunks)
        tail = jnp.zeros((width, 2 * mid), F32) if last else blocks[number + 1][:width, lanes]
        return jnp.concatenate([blocks[number][width:, lanes], tail], axis=0)

    def leave(number):
        c = chunks[number]
        front, rear = slice(0, 2 * mid), slice(2 * mid, 4 * mid)
        level = first_px[number][...]
        above = row_above(first_px, number, front)
        below = row_below(first_px, number, front)
        first_rows[c, :] = jnp.concatenate([jnp.where(low, above, level), below], axis=1).astype(BF16)
        top = row_below(spread_px, number, front)
        centre = pltpu.roll(spread_px[number][:, front], mid, 1)
        bottom = row_above(spread_px, number, rear)
        total = jnp.where(level > 0, (top + centre + bottom) * s_two, 0.0)
        back_ref[c, :] = total[:, :mid].astype(BF16)

    for number in range(len(chunks)):
        to_pixels(number)
    got_out.wait()
    got_x.wait()
    got_params.wait()
    w_third = params_ref[:, c_in + 9 * mid :].astype(BF16)
    w_third = jnp.concatenate([w_third, w_third], axis=0)
    for r in range(3):
        for q in range(3):
            t = 3 * r + q
            taps_ref[q * mid : (q + 1) * mid, r * mid : (r + 1) * mid] = params_ref[
                :, c_in + t * mid : c_in + (t + 1) * mid
            ].astype(BF16)
    for number in range(len(chunks)):
        enter(number)
        if number:
            leave(number - 1)
    leave(len(chunks) - 1)

    spans = [slice(0, pixels)]

    def outer(left, wide, right):
        terms = [
            lax.dot_general(left[k, :wide], right[k, :], (((0,), (0,)), ((), ())), preferred_element_type=F32)
            for k in spans
        ]
        return sum(terms[1:], terms[0])

    even = place_ref[0] % 2 == 0

    def put(grad, column):
        columns = slice(column, column + grad.shape[1])
        for k in range(mid // (2 * rows)):
            lo = 2 * k * rows
            one, two = grad[lo : lo + rows], grad[lo + rows : lo + 2 * rows]
            stream, tile = divmod(k, keep_refs[0].shape[0])
            keep_refs[stream][tile, :, columns] = jnp.where(even, one, two)
            send_refs[stream][tile, :, columns] = jnp.where(even, two, one)

    put(outer(second_bf, mid, out_ref) * (s_three / strips), c_in + 9 * mid)
    grad_two = outer(bs_cols, 3 * mid, first_rows) * (s_two / strips)
    for r in range(3):
        for q in range(3):
            put(grad_two[q * mid : (q + 1) * mid, r * mid : (r + 1) * mid], c_in + (3 * r + q) * mid)
    put(outer(back_ref, mid, x_ref) * (s_one / strips), 0)


def input_grad_kernel(back_ref, out_ref, params_ref, result_ref):
    c_in = out_ref.shape[1]
    w_first = params_ref[:, :c_in].astype(BF16)
    change = jnp.dot(back_ref[...], w_first, preferred_element_type=F32)
    result_ref[...] = (out_ref[...].astype(F32) + (1.0 / math.sqrt(c_in)) * change).astype(BF16)


def update_kernel(
    place_ref, own_speed_ref, other_speed_ref, params_ref, *rest, c_in, mid,
):
    *grads, velocity_ref, weights_ref = rest
    streams = len(grads) // 2
    own_refs, other_refs = grads[:streams], grads[streams:]
    core = place_ref[0] % 2
    pair = place_ref[0] // 2
    tiles, rows, width = own_refs[0].shape
    lane = lax.broadcasted_iota(jnp.int32, (1, 1, width), 2)
    edges = (0, c_in, c_in + 9 * mid, width)

    def column_squares(ref):
        return jnp.sum(jnp.sum(ref[...] ** 2, axis=0, keepdims=True), axis=1, keepdims=True)

    grad_squares = sum(column_squares(ref) for ref in grads)
    param_squares = column_squares(params_ref)
    factor = jnp.zeros((1, 1, width), F32)
    for start, stop in zip(edges[:-1], edges[1:]):
        inside = jnp.logical_and(lane >= start, lane < stop)

        def total(squares):
            return jnp.sum(jnp.where(inside, squares, 0.0), axis=2, keepdims=True)

        trust = jnp.sqrt(total(param_squares)) / (jnp.sqrt(total(grad_squares)) + norm_eps)
        factor = jnp.where(inside, learn_rate * trust, factor)
    factor = factor[0]
    for k in range(tiles * streams):
        for parity, refs, speed in ((core, own_refs, own_speed_ref), (1 - core, other_refs, other_speed_ref)):
            tile = 2 * k + parity
            grad = refs[k // tiles][k % tiles]
            weights_ref[tile] = params_ref[tile] - (momentum * speed[k ^ pair] + factor * grad)
    mine = own_refs[0][pair % tiles]
    for number in range(1, streams):
        mine = jnp.where(pair // tiles == number, own_refs[number][pair % tiles], mine)
    velocity_ref[...] = momentum * own_speed_ref[0] + factor * mine


def full_vmem(count):
    return [pl.BlockSpec(memory_space=pltpu.VMEM) for _ in range(count)]


def in_vmem(*arrays):
    return [pltpu.with_memory_space_constraint(a, pltpu.VMEM) for a in arrays]


def flip(value, axis, bit):
    return lax.ppermute(value, axis, [(i, i ^ bit) for i in range(lax.axis_size(axis))])


def exchange_steps(group, depth):
    across = [(0, 1 << b) for b in range(1, group.bit_length() - 1)]
    along = []
    bit = 1
    while depth % (2 * bit) == 0:
        along.append((1, bit))
        bit *= 2
    steps = []
    for one, two in zip(across, along):
        steps += [(one, two), (two, one)]
    common = min(len(across), len(along))
    steps += [(one, one) for one in across[common:] + along[common:]]
    pairs = []
    for step in steps:
        table = []
        for g in range(group):
            for z in range(depth):
                axis, flipped = step[g % 2]
                to_g, to_z = (g ^ flipped, z) if axis == 0 else (g, z ^ flipped)
                table.append((g * depth + z, to_g * depth + to_z))
        pairs.append(table)
    return pairs, bit


def shards(block_input, mid_first, mid_second, out_grad, params, velocity):
    _, height, width, c_in = block_input.shape
    mid, row = params.shape
    pixels = height * width
    group = lax.axis_size("gx")
    depth = lax.axis_size("gy")
    rows = mid // group
    halves = group // 2
    strips = group * depth
    place = lax.axis_index("gx").reshape(1)
    step = divisor_up_to(height, 8) * width
    streams = 2 if halves % 2 == 0 else 1
    part = pltpu.VMEM((halves // streams, rows, row), F32)

    back_first, out_near, *parts = pl.pallas_call(
        functools.partial(grad_kernel, height=height, width=width, strips=strips, rows=rows, streams=streams),
        out_shape=(pltpu.VMEM((pixels, mid), BF16), pltpu.VMEM((pixels, c_in), BF16), *[part] * (2 * streams)),
        in_specs=[pl.BlockSpec(memory_space=pltpu.SMEM)] + [pl.BlockSpec(memory_space=pltpu.HBM)] * 5,
        out_specs=tuple(full_vmem(2 + 2 * streams)),
        scratch_shapes=[
            pltpu.VMEM((pixels, c_in), BF16),
            pltpu.VMEM((height, width * mid), BF16),
            pltpu.VMEM((height, width * mid), BF16),
            pltpu.VMEM((mid, row), F32),
            pltpu.VMEM((pixels, 4 * mid), BF16),
            pltpu.VMEM((pixels, 4 * mid), BF16),
            pltpu.VMEM((pixels, mid), BF16),
            pltpu.VMEM((4 * mid, 4 * mid), BF16),
            pltpu.SemaphoreType.DMA((5,)),
        ]
        + [
            pltpu.VMEM(shape, F32)
            for shape in ((step, 2 * mid), (step, 2 * mid), (step + 16, 2 * mid), (step, 4 * mid))
            for _ in range(pixels // step)
        ],
        compiler_params=pltpu.CompilerParams(vmem_limit_bytes=28 << 20),
        name="grads",
    )(
        place,
        *(
            pltpu.with_memory_space_constraint(operand, pltpu.HBM)
            for operand in (
                block_input.reshape(pixels, c_in),
                mid_first.reshape(height, width * mid),
                mid_second.reshape(height, width * mid),
                out_grad.reshape(pixels, c_in),
                params,
            )
        ),
    )

    input_grad = pl.pallas_call(
        input_grad_kernel,
        out_shape=pltpu.VMEM((pixels, c_in), BF16),
        in_specs=full_vmem(3),
        out_specs=full_vmem(1)[0],
        cost_estimate=pl.CostEstimate(
            flops=2 * pixels * mid * c_in, bytes_accessed=2 * pixels * (2 * c_in + mid), transcendentals=0
        ),
        compiler_params=pltpu.CompilerParams(vmem_limit_bytes=8 << 20),
        name="input_grad",
    )(*in_vmem(back_first, out_near, params))

    totals = [keep + flip(send, "gx", 1) for keep, send in zip(parts[:streams], parts[streams:])]
    speeds = velocity.reshape(1, rows, row)
    bit = group // 2
    while bit > 1:
        speeds = jnp.stack([speeds, flip(speeds, "gx", bit)], axis=1).reshape(-1, rows, row)
        bit //= 2
    other_speeds = flip(speeds, "gx", 1)
    steps, bit = exchange_steps(group, depth)
    for number, table in enumerate(steps):
        totals = [total + lax.ppermute(total, ("gx", "gy"), table) for total in totals]
        if number == 0:
            totals[0], input_grad = lax.optimization_barrier((totals[0], input_grad))
    for turn in range(1, depth // bit):
        table = [(i, (i + turn * bit) % depth) for i in range(depth)]
        terms = [lax.ppermute(total, "gy", table) for total in totals]
        sums = terms if turn == 1 else [a + b for a, b in zip(sums, terms)]
    if depth > bit:
        totals = [a + b for a, b in zip(totals, sums)]
    others = [flip(total, "gx", 1) for total in totals]

    new_velocity, next_weights = pl.pallas_call(
        functools.partial(update_kernel, c_in=c_in, mid=mid),
        out_shape=(
            jax.ShapeDtypeStruct((rows, row), F32),
            jax.ShapeDtypeStruct((group, rows, row), F32),
        ),
        in_specs=[pl.BlockSpec(memory_space=pltpu.SMEM)] + full_vmem(3 + 2 * streams),
        out_specs=tuple(full_vmem(2)),
        compiler_params=pltpu.CompilerParams(vmem_limit_bytes=8 << 20),
        name="update",
    )(place, *in_vmem(speeds, other_speeds, params.reshape(group, rows, row), *totals, *others))
    return (input_grad.reshape(1, height, width, c_in), new_velocity, next_weights.reshape(mid, row))


def solution(mesh):
    return jax.shard_map(
        shards,
        mesh=mesh,
        in_specs=(
            P(("gx", "gy"), None, None, None),
            P(("gx", "gy"), None, None),
            P(("gx", "gy"), None, None),
            P(("gx", "gy"), None, None, None),
            P(),
            P("gx", None),
        ),
        out_specs=(P(("gx", "gy"), None, None, None), P("gx", None), P()),
        check_vma=False,
    )
```

```python
import functools
import math

import jax
import jax.numpy as jnp
from jax import lax
from jax.experimental import pallas as pl
from jax.experimental.pallas import tpu as pltpu
from jax.sharding import PartitionSpec as P

learn_rate = 0.5
momentum = 0.9
norm_eps = 1e-06

F32 = jnp.float32
BF16 = jnp.bfloat16


def divisor_up_to(number, limit):
    return max(d for d in range(1, limit + 1) if number % d == 0)


def round_up(number, multiple):
    return -(-number // multiple) * multiple


def grad_kernel(
    place_ref, x_hbm, first_hbm, second_hbm, out_hbm, params_hbm,
    back_ref, out_ref, params_ref, *rest, height, width, strips, rows, streams,
):
    keep_refs, send_refs, rest = rest[:streams], rest[streams : 2 * streams], rest[2 * streams :]
    x_ref, first_ref, second_ref, bs_cols, first_rows, taps_ref, arrived, *blocks = rest
    count = len(blocks) // 4
    second_px, first_px, bs_px, spread_px = (blocks[n * count : (n + 1) * count] for n in range(4))
    moves = [
        pltpu.make_async_copy(source, target, arrived.at[n])
        for n, (source, target) in enumerate(
            (
                (params_hbm, params_ref),
                (second_hbm, second_ref),
                (first_hbm, first_ref),
                (out_hbm, out_ref),
                (x_hbm, x_ref),
            )
        )
    ]
    for move in moves[:-1]:
        move.start()
    got_params, got_second, got_first, got_out, got_x = moves
    c_in = x_ref.shape[1]
    mid = params_ref.shape[0]
    pixels = height * width
    pad = 8
    s_one, s_two, s_three = (1.0 / math.sqrt(n) for n in (c_in, 9 * mid, mid))
    block_rows = divisor_up_to(height, 8)
    step = block_rows * width
    chunks = [slice(k * step, (k + 1) * step) for k in range(height // block_rows)]
    low = lax.broadcasted_iota(jnp.int32, (step, 2 * mid), 1) < mid
    low_slab = lax.broadcasted_iota(jnp.int32, (block_rows, 2 * mid), 1) < mid
    column = lax.broadcasted_iota(jnp.int32, (step, 2 * mid), 0) % width

    taps_ref[...] = jnp.zeros_like(taps_ref)
    got_params.wait()
    w_third = params_ref[:, c_in + 9 * mid :].astype(BF16)
    w_third = jnp.concatenate([w_third, w_third], axis=0)
    for r in range(3):
        for q in range(3):
            t = 3 * r + q
            taps_ref[q * mid : (q + 1) * mid, r * mid : (r + 1) * mid] = params_ref[
                :, c_in + t * mid : c_in + (t + 1) * mid
            ].astype(BF16)
    got_second.wait()
    got_first.wait()
    got_x.start()

    def to_pixels(number):
        for ref, px in ((second_ref, second_px[number]), (first_ref, first_px[number])):
            for k in range(width // 2):
                slab = ref[
                    number * block_rows : (number + 1) * block_rows, 2 * mid * k : 2 * mid * (k + 1)
                ].astype(F32)
                turned = pltpu.roll(slab, mid, 1)
                px[pl.ds(2 * k, block_rows, stride=width), :] = jnp.where(low_slab, slab, turned)
                px[pl.ds(2 * k + 1, block_rows, stride=width), :] = jnp.where(low_slab, turned, slab)

    def enter(number):
        c = chunks[number]
        second = second_px[number][...]
        back = lax.dot_general(out_ref[c, :], w_third, (((1,), (1,)), ((), ())), preferred_element_type=F32)
        here = jnp.where(second > 0, back * s_three, 0.0)
        px = bs_px[number]
        px[pad : pad + step, :] = here
        after = jnp.where(column < width - 1, px[pad + 1 : pad + 1 + step, :], 0.0)
        before = jnp.where(column > 0, px[pad - 1 : pad - 1 + step, :], 0.0)
        cols = jnp.concatenate([jnp.where(low, after, here), jnp.where(low, before, second)], axis=1).astype(BF16)
        bs_cols[c, :] = cols
        spread_px[number][...] = jnp.dot(cols, taps_ref[...], preferred_element_type=F32)

    def row_above(blocks, number, lanes):
        head = blocks[number - 1][step - width :, lanes] if number else jnp.zeros((width, 2 * mid), F32)
        return jnp.concatenate([head, blocks[number][: step - width, lanes]], axis=0)

    def row_below(blocks, number, lanes):
        last = number + 1 == len(chunks)
        tail = jnp.zeros((width, 2 * mid), F32) if last else blocks[number + 1][:width, lanes]
        return jnp.concatenate([blocks[number][width:, lanes], tail], axis=0)

    def leave(number):
        c = chunks[number]
        front, rear = slice(0, 2 * mid), slice(2 * mid, 4 * mid)
        level = first_px[number][...]
        above = row_above(first_px, number, front)
        below = row_below(first_px, number, front)
        first_rows[c, :] = jnp.concatenate([jnp.where(low, above, level), below], axis=1).astype(BF16)
        top = row_below(spread_px, number, front)
        centre = pltpu.roll(spread_px[number][:, front], mid, 1)
        bottom = row_above(spread_px, number, rear)
        total = jnp.where(level > 0, (top + centre + bottom) * s_two, 0.0)
        back_ref[c, :] = total[:, :mid].astype(BF16)

    for number in range(len(chunks)):
        to_pixels(number)
    got_out.wait()
    for number in range(len(chunks)):
        enter(number)
        if number:
            leave(number - 1)
    leave(len(chunks) - 1)

    def outer(turned, right):
        return jnp.dot(turned, right, preferred_element_type=F32)

    even = place_ref[0] % 2 == 0

    def put(grad, column):
        columns = slice(column, column + grad.shape[1])
        for k in range(mid // (2 * rows)):
            lo = 2 * k * rows
            one, two = grad[lo : lo + rows], grad[lo + rows : lo + 2 * rows]
            stream, tile = divmod(k, keep_refs[0].shape[0])
            keep_refs[stream][tile, :, columns] = jnp.where(even, one, two)
            send_refs[stream][tile, :, columns] = jnp.where(even, two, one)

    got_x.wait()
    turned = bs_cols[...].T
    put(outer(turned[3 * mid :], out_ref[...]) * (s_three / strips), c_in + 9 * mid)
    grad_two = outer(turned[: 3 * mid], first_rows[...]) * (s_two / strips)
    for r in range(3):
        for q in range(3):
            put(grad_two[q * mid : (q + 1) * mid, r * mid : (r + 1) * mid], c_in + (3 * r + q) * mid)
    put(outer(back_ref[...].T, x_ref[...]) * (s_one / strips), 0)


def input_grad_kernel(back_ref, out_ref, params_ref, result_ref):
    c_in = out_ref.shape[1]
    w_first = params_ref[:, :c_in].astype(BF16)
    change = jnp.dot(back_ref[...], w_first, preferred_element_type=F32)
    result_ref[...] = (out_ref[...].astype(F32) + (1.0 / math.sqrt(c_in)) * change).astype(BF16)


def update_kernel(
    place_ref, own_speed_ref, other_speed_ref, params_ref, *rest, c_in, mid,
):
    *grads, velocity_ref, weights_ref = rest
    streams = len(grads) // 2
    own_refs, other_refs = grads[:streams], grads[streams:]
    core = place_ref[0] % 2
    pair = place_ref[0] // 2
    tiles, rows, width = own_refs[0].shape
    lane = lax.broadcasted_iota(jnp.int32, (1, 1, width), 2)
    edges = (0, c_in, c_in + 9 * mid, width)

    def column_squares(ref):
        return jnp.sum(jnp.sum(ref[...] ** 2, axis=0, keepdims=True), axis=1, keepdims=True)

    grad_squares = sum(column_squares(ref) for ref in grads)
    param_squares = column_squares(params_ref)
    factor = jnp.zeros((1, 1, width), F32)
    for start, stop in zip(edges[:-1], edges[1:]):
        inside = jnp.logical_and(lane >= start, lane < stop)

        def total(squares):
            return jnp.sum(jnp.where(inside, squares, 0.0), axis=2, keepdims=True)

        trust = jnp.sqrt(total(param_squares)) / (jnp.sqrt(total(grad_squares)) + norm_eps)
        factor = jnp.where(inside, learn_rate * trust, factor)
    factor = factor[0]
    for k in range(tiles * streams):
        for parity, refs, speed in ((core, own_refs, own_speed_ref), (1 - core, other_refs, other_speed_ref)):
            tile = 2 * k + parity
            grad = refs[k // tiles][k % tiles]
            weights_ref[tile] = params_ref[tile] - (momentum * speed[k ^ pair] + factor * grad)
    mine = own_refs[0][pair % tiles]
    for number in range(1, streams):
        mine = jnp.where(pair // tiles == number, own_refs[number][pair % tiles], mine)
    velocity_ref[...] = momentum * own_speed_ref[0] + factor * mine


def full_vmem(count):
    return [pl.BlockSpec(memory_space=pltpu.VMEM) for _ in range(count)]


def in_vmem(*arrays):
    return [pltpu.with_memory_space_constraint(a, pltpu.VMEM) for a in arrays]


def flip(value, axis, bit):
    return lax.ppermute(value, axis, [(i, i ^ bit) for i in range(lax.axis_size(axis))])


def exchange_steps(group, depth):
    across = [(0, 1 << b) for b in range(1, group.bit_length() - 1)]
    along = []
    bit = 1
    while depth % (2 * bit) == 0:
        along.append((1, bit))
        bit *= 2
    steps = []
    for one, two in zip(across, along):
        steps += [(one, two), (two, one)]
    common = min(len(across), len(along))
    steps += [(one, one) for one in across[common:] + along[common:]]
    pairs = []
    for step in steps:
        table = []
        for g in range(group):
            for z in range(depth):
                axis, flipped = step[g % 2]
                to_g, to_z = (g ^ flipped, z) if axis == 0 else (g, z ^ flipped)
                table.append((g * depth + z, to_g * depth + to_z))
        pairs.append(table)
    return pairs, bit


def shards(block_input, mid_first, mid_second, out_grad, params, velocity):
    _, height, width, c_in = block_input.shape
    mid, row = params.shape
    pixels = height * width
    group = lax.axis_size("gx")
    depth = lax.axis_size("gy")
    rows = mid // group
    halves = group // 2
    strips = group * depth
    place = lax.axis_index("gx").reshape(1)
    step = divisor_up_to(height, 8) * width
    streams = 2 if halves % 2 == 0 else 1
    part = pltpu.VMEM((halves // streams, rows, row), F32)

    back_first, out_near, params_near, *parts = pl.pallas_call(
        functools.partial(grad_kernel, height=height, width=width, strips=strips, rows=rows, streams=streams),
        out_shape=(pltpu.VMEM((pixels, mid), BF16), pltpu.VMEM((pixels, c_in), BF16), pltpu.VMEM((mid, row), F32), *[part] * (2 * streams)),
        in_specs=[pl.BlockSpec(memory_space=pltpu.SMEM)] + [pl.BlockSpec(memory_space=pltpu.HBM)] * 5,
        out_specs=tuple(full_vmem(3 + 2 * streams)),
        scratch_shapes=[
            pltpu.VMEM((pixels, c_in), BF16),
            pltpu.VMEM((height, width * mid), BF16),
            pltpu.VMEM((height, width * mid), BF16),
            pltpu.VMEM((pixels, 4 * mid), BF16),
            pltpu.VMEM((pixels, 4 * mid), BF16),
            pltpu.VMEM((4 * mid, 4 * mid), BF16),
            pltpu.SemaphoreType.DMA((5,)),
        ]
        + [
            pltpu.VMEM(shape, F32)
            for shape in ((step, 2 * mid), (step, 2 * mid), (step + 16, 2 * mid), (step, 4 * mid))
            for _ in range(pixels // step)
        ],
        compiler_params=pltpu.CompilerParams(vmem_limit_bytes=28 << 20),
        name="grads",
    )(
        place,
        *(
            pltpu.with_memory_space_constraint(operand, pltpu.HBM)
            for operand in (
                block_input.reshape(pixels, c_in),
                mid_first.reshape(height, width * mid),
                mid_second.reshape(height, width * mid),
                out_grad.reshape(pixels, c_in),
                params,
            )
        ),
    )

    input_grad = pl.pallas_call(
        input_grad_kernel,
        out_shape=jax.ShapeDtypeStruct((pixels, c_in), BF16),
        in_specs=full_vmem(3),
        out_specs=full_vmem(1)[0],
        cost_estimate=pl.CostEstimate(
            flops=2 * pixels * mid * c_in, bytes_accessed=2 * pixels * (2 * c_in + mid), transcendentals=0
        ),
        compiler_params=pltpu.CompilerParams(vmem_limit_bytes=8 << 20),
        name="input_grad",
    )(*in_vmem(back_first, out_near, params_near))

    totals = [keep + flip(send, "gx", 1) for keep, send in zip(parts[:streams], parts[streams:])]
    speeds = velocity.reshape(1, rows, row)
    bit = group // 2
    while bit > 1:
        speeds = jnp.stack([speeds, flip(speeds, "gx", bit)], axis=1).reshape(-1, rows, row)
        bit //= 2
    other_speeds = flip(speeds, "gx", 1)
    steps, bit = exchange_steps(group, depth)
    for number, table in enumerate(steps):
        totals = [total + lax.ppermute(total, ("gx", "gy"), table) for total in totals]
        if number + 1 == len(steps):
            totals[-1], input_grad = lax.optimization_barrier((totals[-1], input_grad))
    for turn in range(1, depth // bit):
        table = [(i, (i + turn * bit) % depth) for i in range(depth)]
        terms = [lax.ppermute(total, "gy", table) for total in totals]
        sums = terms if turn == 1 else [a + b for a, b in zip(sums, terms)]
    if depth > bit:
        totals = [a + b for a, b in zip(totals, sums)]
    others = [flip(total, "gx", 1) for total in totals]

    new_velocity, next_weights = pl.pallas_call(
        functools.partial(update_kernel, c_in=c_in, mid=mid),
        out_shape=(
            jax.ShapeDtypeStruct((rows, row), F32),
            jax.ShapeDtypeStruct((group, rows, row), F32),
        ),
        in_specs=[pl.BlockSpec(memory_space=pltpu.SMEM)] + full_vmem(3 + 2 * streams),
        out_specs=tuple(full_vmem(2)),
        compiler_params=pltpu.CompilerParams(vmem_limit_bytes=8 << 20),
        name="update",
    )(place, *in_vmem(speeds, other_speeds, params_near.reshape(group, rows, row), *totals, *others))
    return (input_grad.reshape(1, height, width, c_in), new_velocity, next_weights.reshape(mid, row))


def solution(mesh):
    return jax.shard_map(
        shards,
        mesh=mesh,
        in_specs=(
            P(("gx", "gy"), None, None, None),
            P(("gx", "gy"), None, None),
            P(("gx", "gy"), None, None),
            P(("gx", "gy"), None, None, None),
            P(),
            P("gx", None),
        ),
        out_specs=(P(("gx", "gy"), None, None, None), P("gx", None), P()),
        check_vma=False,
    )
```

```python
import functools
import math

import jax
import jax.numpy as jnp
from jax import lax
from jax.experimental import pallas as pl
from jax.experimental.pallas import tpu as pltpu
from jax.sharding import PartitionSpec as P

learn_rate = 0.5
momentum = 0.9
norm_eps = 1e-06

F32 = jnp.float32
BF16 = jnp.bfloat16


def divisor_up_to(number, limit):
    return max(d for d in range(1, limit + 1) if number % d == 0)


def round_up(number, multiple):
    return -(-number // multiple) * multiple


def grad_kernel(
    place_ref, x_hbm, first_hbm, second_hbm, out_hbm, params_hbm,
    left_ref, x_ref, out_ref, params_ref, taps_grad_ref,
    first_ref, second_ref, bs_cols, first_rows, taps_ref, arrived, *blocks,
    height, width, strips, rows,
):
    count = len(blocks) // 4
    second_px, first_px, bs_px, spread_px = (blocks[n * count : (n + 1) * count] for n in range(4))
    moves = [
        pltpu.make_async_copy(source, target, arrived.at[n])
        for n, (source, target) in enumerate(
            (
                (params_hbm, params_ref),
                (second_hbm, second_ref),
                (first_hbm, first_ref),
                (out_hbm, out_ref),
                (x_hbm, x_ref),
            )
        )
    ]
    for move in moves[:-1]:
        move.start()
    got_params, got_second, got_first, got_out, got_x = moves
    c_in = x_ref.shape[1]
    mid = params_ref.shape[0]
    pixels = height * width
    pad = 8
    s_two, s_three = 1.0 / math.sqrt(9 * mid), 1.0 / math.sqrt(mid)
    block_rows = divisor_up_to(height, 8)
    step = block_rows * width
    chunks = [slice(k * step, (k + 1) * step) for k in range(height // block_rows)]
    low = lax.broadcasted_iota(jnp.int32, (step, 2 * mid), 1) < mid
    low_slab = lax.broadcasted_iota(jnp.int32, (block_rows, 2 * mid), 1) < mid
    column = lax.broadcasted_iota(jnp.int32, (step, 2 * mid), 0) % width

    taps_ref[...] = jnp.zeros_like(taps_ref)
    got_params.wait()
    w_third = params_ref[:, c_in + 9 * mid :].astype(BF16)
    w_third = jnp.concatenate([w_third, w_third], axis=0)
    for r, place in enumerate((1, 0, 3)):
        for q in range(3):
            t = 3 * r + q
            taps_ref[q * mid : (q + 1) * mid, place * mid : (place + 1) * mid] = params_ref[
                :, c_in + t * mid : c_in + (t + 1) * mid
            ].astype(BF16)
    got_second.wait()
    got_first.wait()
    got_x.start()

    def to_pixels(number):
        for ref, px in ((second_ref, second_px[number]), (first_ref, first_px[number])):
            for k in range(width // 2):
                slab = ref[
                    number * block_rows : (number + 1) * block_rows, 2 * mid * k : 2 * mid * (k + 1)
                ].astype(F32)
                turned = pltpu.roll(slab, mid, 1)
                px[pl.ds(2 * k, block_rows, stride=width), :] = jnp.where(low_slab, slab, turned)
                px[pl.ds(2 * k + 1, block_rows, stride=width), :] = jnp.where(low_slab, turned, slab)

    def enter(number):
        c = chunks[number]
        second = second_px[number][...]
        back = lax.dot_general(out_ref[c, :], w_third, (((1,), (1,)), ((), ())), preferred_element_type=F32)
        here = jnp.where(second > 0, back * s_three, 0.0)
        px = bs_px[number]
        px[pad : pad + step, :] = here
        after = jnp.where(column < width - 1, px[pad + 1 : pad + 1 + step, :], 0.0)
        before = jnp.where(column > 0, px[pad - 1 : pad - 1 + step, :], 0.0)
        cols = jnp.concatenate([jnp.where(low, after, here), before], axis=1).astype(BF16)
        bs_cols[c, :] = cols
        spread_px[number][...] = jnp.dot(cols, taps_ref[...], preferred_element_type=F32)

    def row_above(blocks, number, lanes):
        head = blocks[number - 1][step - width :, lanes] if number else jnp.zeros((width, 2 * mid), F32)
        return jnp.concatenate([head, blocks[number][: step - width, lanes]], axis=0)

    def row_below(blocks, number, lanes):
        last = number + 1 == len(chunks)
        tail = jnp.zeros((width, 2 * mid), F32) if last else blocks[number + 1][:width, lanes]
        return jnp.concatenate([blocks[number][width:, lanes], tail], axis=0)

    def leave(number):
        c = chunks[number]
        front, rear = slice(0, 2 * mid), slice(2 * mid, 4 * mid)
        level = first_px[number][...]
        above = row_above(first_px, number, front)
        below = row_below(first_px, number, front)
        first_rows[c, :] = jnp.concatenate([jnp.where(low, above, level), below], axis=1).astype(BF16)
        top = row_below(spread_px, number, front)
        centre = pltpu.roll(spread_px[number][:, front], mid, 1)
        bottom = row_above(spread_px, number, rear)
        total = jnp.where(level > 0, (top + centre + bottom) * s_two, 0.0)
        left_ref[c, :] = jnp.where(low, second_px[number][...], total).astype(BF16)

    for number in range(len(chunks)):
        to_pixels(number)
    got_out.wait()
    for number in range(len(chunks)):
        enter(number)
        if number:
            leave(number - 1)
    leave(len(chunks) - 1)

    taps_grad_ref[...] = jnp.dot(bs_cols[...].T[: 3 * mid], first_rows[...], preferred_element_type=F32) * (
        s_two / strips
    )
    got_x.wait()


def outer_kernel(place_ref, left_ref, x_ref, out_ref, taps_grad_ref, *halves, strips, rows):
    keep_refs, send_refs = halves[: len(halves) // 2], halves[len(halves) // 2 :]
    c_in = x_ref.shape[1]
    mid = left_ref.shape[1] // 2
    even = place_ref[0] % 2 == 0

    def put(grad, column):
        columns = slice(column, column + grad.shape[1])
        for k in range(mid // (2 * rows)):
            lo = 2 * k * rows
            one, two = grad[lo : lo + rows], grad[lo + rows : lo + 2 * rows]
            stream, tile = divmod(k, keep_refs[0].shape[0])
            keep_refs[stream][tile, :, columns] = jnp.where(even, one, two)
            send_refs[stream][tile, :, columns] = jnp.where(even, two, one)

    for r in range(3):
        for q in range(3):
            tap = taps_grad_ref[q * mid : (q + 1) * mid, r * mid : (r + 1) * mid]
            put(tap, c_in + (3 * r + q) * mid)
    turned = left_ref[...].T
    third = jnp.dot(turned[:mid], out_ref[...], preferred_element_type=F32)
    put(third * (1.0 / math.sqrt(mid) / strips), c_in + 9 * mid)
    first = jnp.dot(turned[mid:], x_ref[...], preferred_element_type=F32)
    put(first * (1.0 / math.sqrt(c_in) / strips), 0)


def input_grad_kernel(left_ref, out_ref, params_ref, result_ref):
    c_in = out_ref.shape[1]
    w_first = params_ref[:, :c_in].astype(BF16)
    w_first = jnp.concatenate([jnp.zeros_like(w_first), w_first], axis=0)
    change = jnp.dot(left_ref[...], w_first, preferred_element_type=F32)
    result_ref[...] = (out_ref[...].astype(F32) + (1.0 / math.sqrt(c_in)) * change).astype(BF16)


def update_kernel(
    place_ref, own_speed_ref, other_speed_ref, params_ref, *rest, c_in, mid,
):
    *grads, velocity_ref, weights_ref = rest
    streams = len(grads) // 2
    own_refs, other_refs = grads[:streams], grads[streams:]
    core = place_ref[0] % 2
    pair = place_ref[0] // 2
    tiles, rows, width = own_refs[0].shape
    lane = lax.broadcasted_iota(jnp.int32, (1, 1, width), 2)
    edges = (0, c_in, c_in + 9 * mid, width)

    def column_squares(ref):
        return jnp.sum(jnp.sum(ref[...] ** 2, axis=0, keepdims=True), axis=1, keepdims=True)

    grad_squares = sum(column_squares(ref) for ref in grads)
    param_squares = column_squares(params_ref)
    factor = jnp.zeros((1, 1, width), F32)
    for start, stop in zip(edges[:-1], edges[1:]):
        inside = jnp.logical_and(lane >= start, lane < stop)

        def total(squares):
            return jnp.sum(jnp.where(inside, squares, 0.0), axis=2, keepdims=True)

        trust = jnp.sqrt(total(param_squares)) / (jnp.sqrt(total(grad_squares)) + norm_eps)
        factor = jnp.where(inside, learn_rate * trust, factor)
    factor = factor[0]
    for k in range(tiles * streams):
        for parity, refs, speed in ((core, own_refs, own_speed_ref), (1 - core, other_refs, other_speed_ref)):
            tile = 2 * k + parity
            grad = refs[k // tiles][k % tiles]
            weights_ref[tile] = params_ref[tile] - (momentum * speed[k ^ pair] + factor * grad)
    mine = own_refs[0][pair % tiles]
    for number in range(1, streams):
        mine = jnp.where(pair // tiles == number, own_refs[number][pair % tiles], mine)
    velocity_ref[...] = momentum * own_speed_ref[0] + factor * mine


def full_vmem(count):
    return [pl.BlockSpec(memory_space=pltpu.VMEM) for _ in range(count)]


def in_vmem(*arrays):
    return [pltpu.with_memory_space_constraint(a, pltpu.VMEM) for a in arrays]


def flip(value, axis, bit):
    return lax.ppermute(value, axis, [(i, i ^ bit) for i in range(lax.axis_size(axis))])


def exchange_steps(group, depth):
    across = [(0, 1 << b) for b in range(1, group.bit_length() - 1)]
    along = []
    bit = 1
    while depth % (2 * bit) == 0:
        along.append((1, bit))
        bit *= 2
    steps = []
    for one, two in zip(across, along):
        steps += [(one, two), (two, one)]
    common = min(len(across), len(along))
    steps += [(one, one) for one in across[common:] + along[common:]]
    pairs = []
    for step in steps:
        table = []
        for g in range(group):
            for z in range(depth):
                axis, flipped = step[g % 2]
                to_g, to_z = (g ^ flipped, z) if axis == 0 else (g, z ^ flipped)
                table.append((g * depth + z, to_g * depth + to_z))
        pairs.append(table)
    return pairs, bit


def shards(block_input, mid_first, mid_second, out_grad, params, velocity):
    _, height, width, c_in = block_input.shape
    mid, row = params.shape
    pixels = height * width
    group = lax.axis_size("gx")
    depth = lax.axis_size("gy")
    rows = mid // group
    halves = group // 2
    strips = group * depth
    place = lax.axis_index("gx").reshape(1)
    step = divisor_up_to(height, 8) * width
    streams = 2 if halves % 2 == 0 else 1
    part = pltpu.VMEM((halves // streams, rows, row), F32)
    flat = pltpu.VMEM((pixels, c_in), BF16)

    left, x_near, out_near, params_near, taps_grad = pl.pallas_call(
        functools.partial(grad_kernel, height=height, width=width, strips=strips, rows=rows),
        out_shape=(
            pltpu.VMEM((pixels, 2 * mid), BF16),
            flat,
            flat,
            pltpu.VMEM((mid, row), F32),
            pltpu.VMEM((3 * mid, 4 * mid), F32),
        ),
        in_specs=[pl.BlockSpec(memory_space=pltpu.SMEM)] + [pl.BlockSpec(memory_space=pltpu.HBM)] * 5,
        out_specs=tuple(full_vmem(5)),
        scratch_shapes=[
            pltpu.VMEM((height, width * mid), BF16),
            pltpu.VMEM((height, width * mid), BF16),
            pltpu.VMEM((pixels, 4 * mid), BF16),
            pltpu.VMEM((pixels, 4 * mid), BF16),
            pltpu.VMEM((4 * mid, 4 * mid), BF16),
            pltpu.SemaphoreType.DMA((5,)),
        ]
        + [
            pltpu.VMEM(shape, F32)
            for shape in ((step, 2 * mid), (step, 2 * mid), (step + 16, 2 * mid), (step, 4 * mid))
            for _ in range(pixels // step)
        ],
        compiler_params=pltpu.CompilerParams(vmem_limit_bytes=28 << 20),
        name="grads",
    )(
        place,
        *(
            pltpu.with_memory_space_constraint(operand, pltpu.HBM)
            for operand in (
                block_input.reshape(pixels, c_in),
                mid_first.reshape(height, width * mid),
                mid_second.reshape(height, width * mid),
                out_grad.reshape(pixels, c_in),
                params,
            )
        ),
    )

    parts = pl.pallas_call(
        functools.partial(outer_kernel, strips=strips, rows=rows),
        out_shape=(part,) * (2 * streams),
        in_specs=[pl.BlockSpec(memory_space=pltpu.SMEM)] + full_vmem(4),
        out_specs=tuple(full_vmem(2 * streams)),
        compiler_params=pltpu.CompilerParams(vmem_limit_bytes=8 << 20),
        cost_estimate=pl.CostEstimate(
            flops=4 * pixels * mid * c_in, bytes_accessed=4 * pixels * (c_in + mid), transcendentals=0
        ),
        name="sides",
    )(place, *in_vmem(left, x_near, out_near, taps_grad))

    input_grad = pl.pallas_call(
        input_grad_kernel,
        out_shape=jax.ShapeDtypeStruct((pixels, c_in), BF16),
        in_specs=full_vmem(3),
        out_specs=full_vmem(1)[0],
        cost_estimate=pl.CostEstimate(
            flops=2 * pixels * mid * c_in, bytes_accessed=2 * pixels * (2 * c_in + mid), transcendentals=0
        ),
        compiler_params=pltpu.CompilerParams(vmem_limit_bytes=8 << 20),
        name="input_grad",
    )(*in_vmem(left, out_near, params_near))

    totals = [keep + flip(send, "gx", 1) for keep, send in zip(parts[:streams], parts[streams:])]
    speeds = velocity.reshape(1, rows, row)
    bit = group // 2
    while bit > 1:
        speeds = jnp.stack([speeds, flip(speeds, "gx", bit)], axis=1).reshape(-1, rows, row)
        bit //= 2
    other_speeds = flip(speeds, "gx", 1)
    steps, bit = exchange_steps(group, depth)
    for number, table in enumerate(steps):
        totals = [total + lax.ppermute(total, ("gx", "gy"), table) for total in totals]
        if number + 1 == len(steps):
            totals[-1], input_grad = lax.optimization_barrier((totals[-1], input_grad))
    for turn in range(1, depth // bit):
        table = [(i, (i + turn * bit) % depth) for i in range(depth)]
        terms = [lax.ppermute(total, "gy", table) for total in totals]
        sums = terms if turn == 1 else [a + b for a, b in zip(sums, terms)]
    if depth > bit:
        totals = [a + b for a, b in zip(totals, sums)]
    others = [flip(total, "gx", 1) for total in totals]

    new_velocity, next_weights = pl.pallas_call(
        functools.partial(update_kernel, c_in=c_in, mid=mid),
        out_shape=(
            jax.ShapeDtypeStruct((rows, row), F32),
            jax.ShapeDtypeStruct((group, rows, row), F32),
        ),
        in_specs=[pl.BlockSpec(memory_space=pltpu.SMEM)] + full_vmem(3 + 2 * streams),
        out_specs=tuple(full_vmem(2)),
        compiler_params=pltpu.CompilerParams(vmem_limit_bytes=8 << 20),
        name="update",
    )(place, *in_vmem(speeds, other_speeds, params_near.reshape(group, rows, row), *totals, *others))
    return (input_grad.reshape(1, height, width, c_in), new_velocity, next_weights.reshape(mid, row))


def solution(mesh):
    return jax.shard_map(
        shards,
        mesh=mesh,
        in_specs=(
            P(("gx", "gy"), None, None, None),
            P(("gx", "gy"), None, None),
            P(("gx", "gy"), None, None),
            P(("gx", "gy"), None, None, None),
            P(),
            P("gx", None),
        ),
        out_specs=(P(("gx", "gy"), None, None, None), P("gx", None), P()),
        check_vma=False,
    )
```

```python
import functools
import math

import jax
import jax.numpy as jnp
from jax import lax
from jax.experimental import pallas as pl
from jax.experimental.pallas import tpu as pltpu
from jax.sharding import PartitionSpec as P

learn_rate = 0.5
momentum = 0.9
norm_eps = 1e-06

F32 = jnp.float32
BF16 = jnp.bfloat16


def divisor_up_to(number, limit):
    return max(d for d in range(1, limit + 1) if number % d == 0)


def round_up(number, multiple):
    return -(-number // multiple) * multiple


def grad_kernel(
    place_ref, x_hbm, first_hbm, second_hbm, out_hbm, params_hbm,
    left_ref, x_ref, out_ref, params_ref, taps_grad_ref,
    first_ref, second_ref, bs_cols, first_rows, taps_ref, arrived, *blocks,
    height, width, strips, rows,
):
    count = len(blocks) // 4
    second_px, first_px, bs_px, spread_px = (blocks[n * count : (n + 1) * count] for n in range(4))
    moves = [
        pltpu.make_async_copy(source, target, arrived.at[n])
        for n, (source, target) in enumerate(
            (
                (params_hbm, params_ref),
                (second_hbm, second_ref),
                (first_hbm, first_ref),
                (out_hbm, out_ref),
                (x_hbm, x_ref),
            )
        )
    ]
    for move in moves[:-1]:
        move.start()
    got_params, got_second, got_first, got_out, got_x = moves
    c_in = x_ref.shape[1]
    mid = params_ref.shape[0]
    pixels = height * width
    pad = 8
    s_two, s_three = 1.0 / math.sqrt(9 * mid), 1.0 / math.sqrt(mid)
    block_rows = divisor_up_to(height, 8)
    step = block_rows * width
    chunks = [slice(k * step, (k + 1) * step) for k in range(height // block_rows)]
    low = lax.broadcasted_iota(jnp.int32, (step, 2 * mid), 1) < mid
    low_slab = lax.broadcasted_iota(jnp.int32, (block_rows, 2 * mid), 1) < mid
    column = lax.broadcasted_iota(jnp.int32, (step, 2 * mid), 0) % width

    taps_ref[...] = jnp.zeros_like(taps_ref)
    got_params.wait()
    w_third = params_ref[:, c_in + 9 * mid :].astype(BF16)
    w_third = jnp.concatenate([w_third, w_third], axis=0)
    for r, place in enumerate((1, 0, 3)):
        for q in range(3):
            t = 3 * r + q
            taps_ref[q * mid : (q + 1) * mid, place * mid : (place + 1) * mid] = params_ref[
                :, c_in + t * mid : c_in + (t + 1) * mid
            ].astype(BF16)
    got_second.wait()
    got_first.wait()
    got_x.start()

    def to_pixels(number):
        for ref, px in ((second_ref, second_px[number]), (first_ref, first_px[number])):
            for k in range(width // 2):
                slab = ref[
                    number * block_rows : (number + 1) * block_rows, 2 * mid * k : 2 * mid * (k + 1)
                ].astype(F32)
                turned = pltpu.roll(slab, mid, 1)
                px[pl.ds(2 * k, block_rows, stride=width), :] = jnp.where(low_slab, slab, turned)
                px[pl.ds(2 * k + 1, block_rows, stride=width), :] = jnp.where(low_slab, turned, slab)

    def enter(number):
        c = chunks[number]
        second = second_px[number][...]
        back = lax.dot_general(out_ref[c, :], w_third, (((1,), (1,)), ((), ())), preferred_element_type=F32)
        here = jnp.where(second > 0, back * s_three, 0.0)
        px = bs_px[number]
        px[pad : pad + step, :] = here
        after = jnp.where(column < width - 1, px[pad + 1 : pad + 1 + step, :], 0.0)
        before = jnp.where(column > 0, px[pad - 1 : pad - 1 + step, :], 0.0)
        cols = jnp.concatenate([jnp.where(low, after, here), before], axis=1).astype(BF16)
        bs_cols[c, :] = cols
        spread_px[number][...] = jnp.dot(cols, taps_ref[...], preferred_element_type=F32)

    def row_above(blocks, number, lanes):
        head = blocks[number - 1][step - width :, lanes] if number else jnp.zeros((width, 2 * mid), F32)
        return jnp.concatenate([head, blocks[number][: step - width, lanes]], axis=0)

    def row_below(blocks, number, lanes):
        last = number + 1 == len(chunks)
        tail = jnp.zeros((width, 2 * mid), F32) if last else blocks[number + 1][:width, lanes]
        return jnp.concatenate([blocks[number][width:, lanes], tail], axis=0)

    def leave(number):
        c = chunks[number]
        front, rear = slice(0, 2 * mid), slice(2 * mid, 4 * mid)
        level = first_px[number][...]
        above = row_above(first_px, number, front)
        below = row_below(first_px, number, front)
        first_rows[c, :] = jnp.concatenate([jnp.where(low, above, level), below], axis=1).astype(BF16)
        top = row_below(spread_px, number, front)
        centre = pltpu.roll(spread_px[number][:, front], mid, 1)
        bottom = row_above(spread_px, number, rear)
        total = jnp.where(level > 0, (top + centre + bottom) * s_two, 0.0)
        left_ref[c, :] = jnp.where(low, second_px[number][...], total).astype(BF16)

    for number in range(len(chunks)):
        to_pixels(number)
    got_out.wait()
    for number in range(len(chunks)):
        enter(number)
        if number:
            leave(number - 1)
    leave(len(chunks) - 1)

    taps_grad_ref[...] = jnp.dot(bs_cols[...].T[: 3 * mid], first_rows[...], preferred_element_type=F32) * (
        s_two / strips
    )
    got_x.wait()


def outer_kernel(place_ref, left_ref, x_ref, out_ref, taps_grad_ref, *halves, strips, rows):
    keep_refs, send_refs = halves[: len(halves) // 2], halves[len(halves) // 2 :]
    c_in = x_ref.shape[1]
    mid = left_ref.shape[1] // 2
    even = place_ref[0] % 2 == 0

    def put(grad, column):
        columns = slice(column, column + grad.shape[1])
        for k in range(mid // (2 * rows)):
            lo = 2 * k * rows
            one, two = grad[lo : lo + rows], grad[lo + rows : lo + 2 * rows]
            stream, tile = divmod(k, keep_refs[0].shape[0])
            keep_refs[stream][tile, :, columns] = jnp.where(even, one, two)
            send_refs[stream][tile, :, columns] = jnp.where(even, two, one)

    for r in range(3):
        for q in range(3):
            tap = taps_grad_ref[q * mid : (q + 1) * mid, r * mid : (r + 1) * mid]
            put(tap, c_in + (3 * r + q) * mid)
    turned = left_ref[...].T
    third = jnp.dot(turned[:mid], out_ref[...], preferred_element_type=F32)
    put(third * (1.0 / math.sqrt(mid) / strips), c_in + 9 * mid)
    first = jnp.dot(turned[mid:], x_ref[...], preferred_element_type=F32)
    put(first * (1.0 / math.sqrt(c_in) / strips), 0)


def input_grad_kernel(left_ref, out_ref, params_ref, result_ref):
    c_in = out_ref.shape[1]
    w_first = params_ref[:, :c_in].astype(BF16)
    w_first = jnp.concatenate([jnp.zeros_like(w_first), w_first], axis=0)
    change = jnp.dot(left_ref[...], w_first, preferred_element_type=F32)
    result_ref[...] = (out_ref[...].astype(F32) + (1.0 / math.sqrt(c_in)) * change).astype(BF16)


def update_kernel(
    place_ref, own_speed_ref, other_speed_ref, params_ref, *rest, c_in, mid,
):
    *grads, velocity_ref, weights_ref = rest
    streams = len(grads) // 2
    own_refs, other_refs = grads[:streams], grads[streams:]
    core = place_ref[0] % 2
    pair = place_ref[0] // 2
    tiles, rows, width = own_refs[0].shape
    lane = lax.broadcasted_iota(jnp.int32, (1, 1, width), 2)
    edges = (0, c_in, c_in + 9 * mid, width)

    def column_squares(ref):
        return jnp.sum(jnp.sum(ref[...] ** 2, axis=0, keepdims=True), axis=1, keepdims=True)

    own_squares, other_squares = (sum(column_squares(ref) for ref in refs) for refs in (own_refs, other_refs))
    grad_squares = own_squares + other_squares
    param_squares = column_squares(params_ref)
    factor = jnp.zeros((1, 1, width), F32)
    for start, stop in zip(edges[:-1], edges[1:]):
        inside = jnp.logical_and(lane >= start, lane < stop)

        def total(squares):
            return jnp.sum(jnp.where(inside, squares, 0.0), axis=2, keepdims=True)

        trust = jnp.sqrt(total(param_squares)) / (jnp.sqrt(total(grad_squares)) + norm_eps)
        factor = jnp.where(inside, learn_rate * trust, factor)
    factor = factor[0]
    for k in range(tiles * streams):
        for parity, refs, speed in ((core, own_refs, own_speed_ref), (1 - core, other_refs, other_speed_ref)):
            tile = 2 * k + parity
            grad = refs[k // tiles][k % tiles]
            weights_ref[tile] = params_ref[tile] - (momentum * speed[k ^ pair] + factor * grad)
    mine = own_refs[0][pair % tiles]
    for number in range(1, streams):
        mine = jnp.where(pair // tiles == number, own_refs[number][pair % tiles], mine)
    velocity_ref[...] = momentum * own_speed_ref[0] + factor * mine


def full_vmem(count):
    return [pl.BlockSpec(memory_space=pltpu.VMEM) for _ in range(count)]


def in_vmem(*arrays):
    return [pltpu.with_memory_space_constraint(a, pltpu.VMEM) for a in arrays]


def flip(value, axis, bit):
    return lax.ppermute(value, axis, [(i, i ^ bit) for i in range(lax.axis_size(axis))])


def exchange_steps(group, depth):
    across = [(0, 1 << b) for b in range(1, group.bit_length() - 1)]
    along = []
    bit = 1
    while depth % (2 * bit) == 0:
        along.append((1, bit))
        bit *= 2
    steps = []
    for one, two in zip(across, along):
        steps += [(one, two), (two, one)]
    common = min(len(across), len(along))
    steps += [(one, one) for one in across[common:] + along[common:]]
    pairs = []
    for step in steps:
        table = []
        for g in range(group):
            for z in range(depth):
                axis, flipped = step[g % 2]
                to_g, to_z = (g ^ flipped, z) if axis == 0 else (g, z ^ flipped)
                table.append((g * depth + z, to_g * depth + to_z))
        pairs.append(table)
    return pairs, bit


def shards(block_input, mid_first, mid_second, out_grad, params, velocity):
    _, height, width, c_in = block_input.shape
    mid, row = params.shape
    pixels = height * width
    group = lax.axis_size("gx")
    depth = lax.axis_size("gy")
    rows = mid // group
    halves = group // 2
    strips = group * depth
    place = lax.axis_index("gx").reshape(1)
    step = divisor_up_to(height, 8) * width
    streams = 2 if halves % 2 == 0 else 1
    part = pltpu.VMEM((halves // streams, rows, row), F32)
    flat = pltpu.VMEM((pixels, c_in), BF16)

    left, x_near, out_near, params_near, taps_grad = pl.pallas_call(
        functools.partial(grad_kernel, height=height, width=width, strips=strips, rows=rows),
        out_shape=(
            pltpu.VMEM((pixels, 2 * mid), BF16),
            flat,
            flat,
            pltpu.VMEM((mid, row), F32),
            pltpu.VMEM((3 * mid, 4 * mid), F32),
        ),
        in_specs=[pl.BlockSpec(memory_space=pltpu.SMEM)] + [pl.BlockSpec(memory_space=pltpu.HBM)] * 5,
        out_specs=tuple(full_vmem(5)),
        scratch_shapes=[
            pltpu.VMEM((height, width * mid), BF16),
            pltpu.VMEM((height, width * mid), BF16),
            pltpu.VMEM((pixels, 4 * mid), BF16),
            pltpu.VMEM((pixels, 4 * mid), BF16),
            pltpu.VMEM((4 * mid, 4 * mid), BF16),
            pltpu.SemaphoreType.DMA((5,)),
        ]
        + [
            pltpu.VMEM(shape, F32)
            for shape in ((step, 2 * mid), (step, 2 * mid), (step + 16, 2 * mid), (step, 4 * mid))
            for _ in range(pixels // step)
        ],
        compiler_params=pltpu.CompilerParams(vmem_limit_bytes=28 << 20),
        name="grads",
    )(
        place,
        *(
            pltpu.with_memory_space_constraint(operand, pltpu.HBM)
            for operand in (
                block_input.reshape(pixels, c_in),
                mid_first.reshape(height, width * mid),
                mid_second.reshape(height, width * mid),
                out_grad.reshape(pixels, c_in),
                params,
            )
        ),
    )

    parts = pl.pallas_call(
        functools.partial(outer_kernel, strips=strips, rows=rows),
        out_shape=(part,) * (2 * streams),
        in_specs=[pl.BlockSpec(memory_space=pltpu.SMEM)] + full_vmem(4),
        out_specs=tuple(full_vmem(2 * streams)),
        compiler_params=pltpu.CompilerParams(vmem_limit_bytes=8 << 20),
        cost_estimate=pl.CostEstimate(
            flops=4 * pixels * mid * c_in, bytes_accessed=4 * pixels * (c_in + mid), transcendentals=0
        ),
        name="sides",
    )(place, *in_vmem(left, x_near, out_near, taps_grad))

    input_grad = pl.pallas_call(
        input_grad_kernel,
        out_shape=jax.ShapeDtypeStruct((pixels, c_in), BF16),
        in_specs=full_vmem(3),
        out_specs=full_vmem(1)[0],
        cost_estimate=pl.CostEstimate(
            flops=2 * pixels * mid * c_in, bytes_accessed=2 * pixels * (2 * c_in + mid), transcendentals=0
        ),
        compiler_params=pltpu.CompilerParams(vmem_limit_bytes=8 << 20),
        name="input_grad",
    )(*in_vmem(left, out_near, params_near))

    totals = [keep + flip(send, "gx", 1) for keep, send in zip(parts[:streams], parts[streams:])]
    speeds = velocity.reshape(1, rows, row)
    bit = group // 2
    while bit > 1:
        speeds = jnp.stack([speeds, flip(speeds, "gx", bit)], axis=1).reshape(-1, rows, row)
        bit //= 2
    other_speeds = flip(speeds, "gx", 1)
    steps, bit = exchange_steps(group, depth)
    for number, table in enumerate(steps):
        totals = [total + lax.ppermute(total, ("gx", "gy"), table) for total in totals]
        if number + 1 == len(steps):
            totals[-1], input_grad = lax.optimization_barrier((totals[-1], input_grad))
    for turn in range(1, depth // bit):
        table = [(i, (i + turn * bit) % depth) for i in range(depth)]
        terms = [lax.ppermute(total, "gy", table) for total in totals]
        sums = terms if turn == 1 else [a + b for a, b in zip(sums, terms)]
    if depth > bit:
        totals = [a + b for a, b in zip(totals, sums)]
    others = [flip(total, "gx", 1) for total in totals]

    new_velocity, next_weights = pl.pallas_call(
        functools.partial(update_kernel, c_in=c_in, mid=mid),
        out_shape=(
            jax.ShapeDtypeStruct((rows, row), F32),
            jax.ShapeDtypeStruct((group, rows, row), F32),
        ),
        in_specs=[pl.BlockSpec(memory_space=pltpu.SMEM)] + full_vmem(3 + 2 * streams),
        out_specs=tuple(full_vmem(2)),
        compiler_params=pltpu.CompilerParams(vmem_limit_bytes=8 << 20),
        name="update",
    )(place, *in_vmem(speeds, other_speeds, params_near.reshape(group, rows, row), *totals, *others))
    return (input_grad.reshape(1, height, width, c_in), new_velocity, next_weights.reshape(mid, row))


def solution(mesh):
    return jax.shard_map(
        shards,
        mesh=mesh,
        in_specs=(
            P(("gx", "gy"), None, None, None),
            P(("gx", "gy"), None, None),
            P(("gx", "gy"), None, None),
            P(("gx", "gy"), None, None, None),
            P(),
            P("gx", None),
        ),
        out_specs=(P(("gx", "gy"), None, None, None), P("gx", None), P()),
        check_vma=False,
    )
```
